32 devices in a mesh: batch: 2 (over y), res: 16 (over z, x, core), head: 1.
Axes of the slice: x: 2, y: 2, z: 4, core: 2. Of those that a mesh axis runs over, the one named last changes fastest.
Arguments:
- single: bfloat16 [768, 384], P(('batch', 'res')), parts along dimension 0, may hold values from -50 to 50
- pair: bfloat16 [768, 384, 128], P(('batch', 'res'), 'head'), parts along dimension 0, may hold values from -6 to 6
- rotations: float32 [3, 3, 768], P(None, None, 'batch'), parts along dimension 2, may hold values from -1 to 1, as said below
- translations: float32 [3, 768], P(None, 'batch'), parts along dimension 1, may hold values from -4 to 4
- residue_chain_index: int32 [384], replicated, may hold values from 0 to 3, never falling along the last dimension, each value on 1 to 192 neighbouring positions
- residue_move_mask: int32 [768], P('batch'), parts along dimension 0, may hold values 0 or 1
- timestep: int32 [1], replicated, may hold values from 0 to 6
- single_projection_weight: bfloat16 [384, 16, 132], P(None, 'head'), may hold values from -1 to 1, as said below
- head_bias_weight: bfloat16 [128, 16], replicated, may hold values from -0.5 to 0.5
- head_distance_weight: float32 [16], P('head'), may hold values from 0.1 to 1
- chain_logit_offset: float32 [16], P('head'), may hold values from -2 to 2
- local_output_weight: bfloat16 [16, 64, 384], P('head'), may hold values from -0.109375 to 0.109375
- pair_output_weight: bfloat16 [16, 128, 384], replicated, may hold values from -0.109375 to 0.109375
- single_norm_gain: float32 [384], replicated, may hold values from 0.5 to 1.5
- frame_velocity_weight: bfloat16 [384, 6], replicated, may hold values from -0.3125 to 0.3125
- left_pair_weight: bfloat16 [384, 128], replicated, may hold values from -0.3125 to 0.3125
- right_pair_weight: bfloat16 [384, 128], replicated, may hold values from -0.3125 to 0.3125
- pair_norm_gain: float32 [128], replicated, may hold values from 0.5 to 1.5
- transition_hidden_weight: bfloat16 [128, 256], replicated, may hold values from -0.5 to 0.5
- transition_middle_weight: bfloat16 [256, 256], replicated, may hold values from -0.375 to 0.375
- transition_back_weight: bfloat16 [256, 128], replicated, may hold values from -0.375 to 0.375
Outputs:
- single_out: bfloat16 [768, 384], P(('batch', 'res')), parts along dimension 0
- rot_out: float32 [3, 3, 768], P(None, None, ('batch', 'res')), parts along dimension 2
- trans_out: float32 [3, 768], P(None, ('batch', 'res')), parts along dimension 1
- pair_out: bfloat16 [768, 384, 128], P(('batch', 'res'), 'head'), parts along dimension 0
The draws below stay inside these ranges and needn't reach their ends.
There are 2 independent parts, one for each index of `batch`. The reference program is written for one: setup_inputs(seed, part) draws one part's arguments, and reference() takes and returns one part's arrays. A program takes and returns all parts, laid end to end along the dimension named above; an argument that names none is the same for every part. Nothing has to cross between parts.
Inputs may be any that keep to these rules, and one draw needn't show every extreme that they name: Each residue's 3 x 3 block rotations[:, :, i] is a rotation matrix. `single_projection_weight`: mean zero entries of deviation about 1 / sqrt(384).
All inputs are finite; a program needn't handle non-finite values.
Results may differ from the reference program's by a relative error of at most 0.0044.
The reference program's roundings to bfloat16 on the way count: a program that leaves them out, or rounds other values in their place, can miss the bound.
Values may be sent and summed in bfloat16 or wider, within the bound.
A program may use at most 64 MiB of HBM per device.

```python
import math
import jax
import jax.numpy as jnp
import numpy as np
from jax import lax

D = 384
HEAD_TOTAL = 16
HEAD_FEATURES = 16
PQ = 8
PV = 12
C_Z = 128
HID = 256
STEPS = 8
RESIDUES = 384
PROJ_FEAT = 132
OUT_FEAT = 64


def draw_single(key, part):
    base = jnp.clip(jax.random.normal(jax.random.fold_in(key, 11), (RESIDUES, D), jnp.float32), -4.0, 4.0)
    return base.astype(jnp.bfloat16)


def axis_turn(angles, axis_name):
    cosine = jnp.cos(angles)
    sine = jnp.sin(angles)
    zeros_row = jnp.zeros_like(angles)
    ones_row = jnp.ones_like(angles)
    if axis_name == 'zaxis':
        return jnp.stack([jnp.stack([cosine, -sine, zeros_row]), jnp.stack([sine, cosine, zeros_row]), jnp.stack([zeros_row, zeros_row, ones_row])])
    return jnp.stack([jnp.stack([cosine, zeros_row, sine]), jnp.stack([zeros_row, ones_row, zeros_row]), jnp.stack([-sine, zeros_row, cosine])])


def draw_rotations(key, part):
    angles = jax.random.uniform(jax.random.fold_in(key, 21), (3, RESIDUES), jnp.float32, -math.pi, math.pi)
    first_turn = axis_turn(angles[0], 'zaxis')
    second_turn = axis_turn(angles[1], 'yaxis')
    third_turn = axis_turn(angles[2], 'zaxis')
    joined = jnp.einsum('abn,bcn->acn', first_turn, second_turn)
    joined = jnp.einsum('abn,bcn->acn', joined, third_turn)
    return jnp.clip(joined, -1.0, 1.0).astype(jnp.float32)


def draw_translations(key, part):
    shifts = jnp.clip(jax.random.normal(jax.random.fold_in(key, 31), (3, RESIDUES), jnp.float32), -4.0, 4.0)
    return shifts.astype(jnp.float32)


def draw_single_projection_weight(key, part):
    span = math.sqrt(3.0 / D)
    weights = jax.random.uniform(jax.random.fold_in(key, 41), (D, HEAD_TOTAL, PROJ_FEAT), jnp.float32, -span, span)
    return weights.astype(jnp.bfloat16)


def with_ends(result, own_key, smallest, high):
    index_at = [jax.random.randint(jax.random.fold_in(own_key, axis), (), 0, length) for axis, length in enumerate(result.shape)]
    longest = result.shape.index(max(result.shape))
    next_to = index_at[:longest] + [(index_at[longest] + 1) % result.shape[longest]] + index_at[longest + 1:]
    return result.at[tuple(index_at)].set(smallest).at[tuple(next_to)].set(high)


def block_levels(rng, shape, split, least, high):
    level = 1.0
    for dim, parts in split:
        draws = jax.random.uniform(jax.random.fold_in(jax.random.fold_in(rng, 6), dim), (parts,), jnp.float32, least / len(split), high / len(split))
        level = level * jnp.repeat(jnp.exp(draws), shape[dim] // parts).reshape((-1,) + (1,) * (len(shape) - 1 - dim))
    return level


def profile(amount, total, limit, lean):
    loads = [(1 << 20) // math.isqrt(grade ** lean) + 1 for grade in range(2, amount + 1)]
    spare, given = total - limit - (amount - 1), [1] * (amount - 1)
    while spare > 0:
        candidates = [i for i in range(amount - 1) if given[i] < limit]
        whole, remaining = sum([loads[i] for i in candidates]), spare
        for i in candidates:
            more = min(limit - given[i], max(1, remaining * loads[i] // whole), spare)
            given[i] = given[i] + more
            spare = spare - more
    return np.array([limit] + given)


def uneven(stream_key, count, total, reach, lean):
    if count == 2:
        one = jax.random.randint(stream_key, (), max(1, total - reach), min(reach, total - 1) + 1)
        return jnp.stack([one, total - one])
    lengths = jnp.asarray(profile(count, total, reach, lean), jnp.int32)
    twos = (count - 1) // 2
    donor, receiver = lengths[1:1 + 2 * twos:2], lengths[2:2 + 2 * twos:2]
    room = jnp.minimum(donor - 1, reach - receiver)
    shifted = jax.random.randint(jax.random.fold_in(stream_key, 1), (twos,), 0, 1 << 20) % (room + 1)
    lengths = lengths.at[1:1 + 2 * twos:2].set(donor - shifted).at[2:2 + 2 * twos:2].set(receiver + shifted)
    return lengths[jax.random.permutation(jax.random.fold_in(stream_key, 2), count)]


def normal_values(own_key, shape, deviation, bound, pieces=(), kind=jnp.bfloat16):
    level = block_levels(own_key, shape, pieces, -0.22, 0.18) if pieces else 1.0
    values = jax.random.normal(own_key, shape, jnp.float32) * deviation * level
    return jnp.minimum(jnp.maximum(values, -bound), bound).astype(kind)


def setup_inputs(seed: int = 0, part: int = 0) -> dict:
    key_of = jax.random.split(jax.random.key(seed), 22)
    part_splits = jax.random.split(jax.random.fold_in(key_of[21], part), 22)
    single = draw_single(jax.random.fold_in(jax.random.fold_in(key_of[21], part), 71), part)
    pair = normal_values(part_splits[1], (RESIDUES, RESIDUES, C_Z), 1.0, 6.0, ((0, 16),))
    rotations = draw_rotations(jax.random.fold_in(jax.random.fold_in(key_of[21], part), 71), part)
    translations = draw_translations(jax.random.fold_in(jax.random.fold_in(key_of[21], part), 71), part)
    residue_chain_index = jnp.searchsorted(jnp.cumsum(uneven(key_of[4], 4, RESIDUES, RESIDUES // 2, 0)), jnp.arange(RESIDUES), side="right").astype(jnp.int32)
    residue_move_mask = with_ends((jax.random.randint(part_splits[5], (RESIDUES,), 0, 8) < 7).astype(jnp.int32), jax.random.fold_in(part_splits[5], 1), 0, 1)
    timestep = jax.random.randint(key_of[6], (1,), 0, STEPS - 1).astype(jnp.int32)
    single_projection_weight = draw_single_projection_weight(jax.random.fold_in(key_of[21], 71), part)
    head_bias_weight = normal_values(key_of[8], (C_Z, HEAD_TOTAL), C_Z ** -0.5, 0.5)
    head_distance_weight = jnp.clip(jnp.exp(jax.random.uniform(key_of[9], (HEAD_TOTAL,), jnp.float32, math.log(0.1), math.log(1.0))), 0.1, 1.0)
    chain_logit_offset = jnp.clip(jax.random.uniform(key_of[10], (HEAD_TOTAL,), jnp.float32, -2.0, 2.0), -2.0, 2.0)
    local_output_weight = normal_values(key_of[11], (HEAD_TOTAL, OUT_FEAT, D), (HEAD_TOTAL * (OUT_FEAT + C_Z)) ** -0.5, 0.109375)
    pair_output_weight = normal_values(key_of[12], (HEAD_TOTAL, C_Z, D), (HEAD_TOTAL * (OUT_FEAT + C_Z)) ** -0.5, 0.109375)
    single_norm_gain = jnp.clip(1.0 + 0.1 * jax.random.normal(key_of[13], (D,), jnp.float32), 0.5, 1.5)
    frame_velocity_weight = normal_values(key_of[14], (D, 6), D ** -0.5, 0.3125)
    left_pair_weight = normal_values(key_of[15], (D, C_Z), D ** -0.5, 0.3125)
    right_pair_weight = normal_values(key_of[16], (D, C_Z), D ** -0.5, 0.3125)
    pair_norm_gain = jnp.clip(1.0 + 0.1 * jax.random.normal(key_of[17], (C_Z,), jnp.float32), 0.5, 1.5)
    transition_hidden_weight = normal_values(key_of[18], (C_Z, HID), C_Z ** -0.5, 0.5)
    transition_middle_weight = normal_values(key_of[19], (HID, HID), HID ** -0.5, 0.375)
    transition_back_weight = normal_values(key_of[20], (HID, C_Z), HID ** -0.5, 0.375)
    return {"single": single, "pair": pair, "rotations": rotations, "translations": translations, "residue_chain_index": residue_chain_index, "residue_move_mask": residue_move_mask, "timestep": timestep, "single_projection_weight": single_projection_weight, "head_bias_weight": head_bias_weight, "head_distance_weight": head_distance_weight, "chain_logit_offset": chain_logit_offset, "local_output_weight": local_output_weight, "pair_output_weight": pair_output_weight, "single_norm_gain": single_norm_gain, "frame_velocity_weight": frame_velocity_weight, "left_pair_weight": left_pair_weight, "right_pair_weight": right_pair_weight, "pair_norm_gain": pair_norm_gain, "transition_hidden_weight": transition_hidden_weight, "transition_middle_weight": transition_middle_weight, "transition_back_weight": transition_back_weight}


LOGIT_FACTOR = math.sqrt(1.0 / 3.0)
HIGHEST = lax.Precision.HIGHEST

def rounded(values):
    return lax.optimization_barrier(values.astype(jnp.bfloat16))

def layer_norm(values, gain):
    centre = lax.optimization_barrier(jnp.mean(values, axis=-1, keepdims=True))
    variance = lax.optimization_barrier(jnp.mean(jnp.square(values - centre), axis=-1, keepdims=True))
    return (values - centre) * lax.rsqrt(variance + 1e-05) * gain

def to_global(local, rot_cols, trans_cols, npoints):
    rows_here = local.shape[0]
    heads_here = local.shape[1]
    points = local.reshape(rows_here, heads_here, npoints, 3)
    turned = lax.optimization_barrier(jnp.sum(rot_cols[:, None, None, :, :] * points[:, :, :, None, :], axis=-1))
    return turned + trans_cols[:, None, None, :]

def hat_matrix(vectors):
    comp_x = vectors[:, 0]
    comp_y = vectors[:, 1]
    comp_z = vectors[:, 2]
    zeros_col = jnp.zeros_like(comp_x)
    first_row = jnp.stack([zeros_col, -comp_z, comp_y], -1)
    second_row = jnp.stack([comp_z, zeros_col, -comp_x], -1)
    third_row = jnp.stack([-comp_y, comp_x, zeros_col], -1)
    return jnp.stack([first_row, second_row, third_row], 1)

def frame_step(single_out, frame_velocity_weight, rot_cols, trans_cols, live_rows, step_ratio):
    motion = jnp.dot(single_out, frame_velocity_weight, preferred_element_type=jnp.float32)
    rotvec = step_ratio * jnp.tanh(motion[:, 0:3]) * live_rows[:, None]
    velocity = step_ratio * motion[:, 3:6] * live_rows[:, None]
    angle_sq = lax.optimization_barrier(jnp.sum(jnp.square(rotvec), -1))
    coef_a = jnp.zeros_like(angle_sq)
    coef_b = jnp.zeros_like(angle_sq)
    coef_c = jnp.zeros_like(angle_sq)
    powers = jnp.ones_like(angle_sq)
    for order in range(8):
        parity = (-1.0) ** order
        coef_a = coef_a + powers * (parity / float(math.factorial(2 * order + 1)))
        coef_b = coef_b + powers * (parity / float(math.factorial(2 * order + 2)))
        coef_c = coef_c + powers * (parity / float(math.factorial(2 * order + 3)))
        powers = powers * angle_sq
    cross_mat = hat_matrix(rotvec)
    cross_sq = jnp.einsum('nab,nbc->nac', cross_mat, cross_mat, precision=HIGHEST)
    identity = jnp.eye(3, dtype=jnp.float32)[None]
    turn = identity + coef_a[:, None, None] * cross_mat + coef_b[:, None, None] * cross_sq
    jacobian = identity + coef_b[:, None, None] * cross_mat + coef_c[:, None, None] * cross_sq
    new_rot = jnp.einsum('nab,nbc->nac', rot_cols, turn, precision=HIGHEST)
    moved = jnp.einsum('nab,nb->na', jacobian, velocity, precision=HIGHEST)
    new_trans = trans_cols + jnp.einsum('nab,nb->na', rot_cols, moved, precision=HIGHEST)
    return (jnp.transpose(new_rot, (1, 2, 0)), jnp.transpose(new_trans))

def reference(single, pair, rotations, translations, residue_chain_index, residue_move_mask, timestep, single_projection_weight, head_bias_weight, head_distance_weight, chain_logit_offset, local_output_weight, pair_output_weight, single_norm_gain, frame_velocity_weight, left_pair_weight, right_pair_weight, pair_norm_gain, transition_hidden_weight, transition_middle_weight, transition_back_weight):
    rot_cols = jnp.transpose(rotations, (2, 0, 1))
    trans_cols = jnp.transpose(translations)
    projected = jnp.einsum('nd,dhf->nhf', single.astype(jnp.float32), single_projection_weight.astype(jnp.float32), precision=HIGHEST)
    query_values = rounded(projected[:, :, 0:HEAD_FEATURES])
    key_float = rounded(projected[:, :, HEAD_FEATURES:2 * HEAD_FEATURES]).astype(jnp.float32)
    value_float = rounded(projected[:, :, 2 * HEAD_FEATURES:3 * HEAD_FEATURES]).astype(jnp.float32)
    offset = 3 * HEAD_FEATURES
    query_points = to_global(projected[:, :, offset:offset + 3 * PQ], rot_cols, trans_cols, PQ)
    key_points = rounded(to_global(projected[:, :, offset + 3 * PQ:offset + 6 * PQ], rot_cols, trans_cols, PQ))
    value_points = rounded(to_global(projected[:, :, offset + 6 * PQ:], rot_cols, trans_cols, PV))
    key_flat = key_points.astype(jnp.float32).reshape(RESIDUES, HEAD_TOTAL, 3 * PQ)
    value_flat = value_points.astype(jnp.float32).reshape(RESIDUES, HEAD_TOTAL, 3 * PV)
    key_square = jnp.transpose(lax.optimization_barrier(jnp.sum(jnp.square(key_flat), -1)))
    key_present = residue_move_mask > 0
    point_term_weight = math.sqrt(2.0 / (9.0 * PQ))
    block_rows = math.gcd(RESIDUES, 128)
    block_count = RESIDUES // block_rows

    def attend(args):
        query_rows, qpoint_rows, pair_rows, rot_rows, trans_rows, chain_rows = args
        scalar_logit_term = jnp.einsum('rhc,nhc->rhn', query_rows.astype(jnp.float32), key_float, precision=HIGHEST)
        query_flattened = qpoint_rows.reshape(block_rows, HEAD_TOTAL, 3 * PQ)
        cross_term = jnp.einsum('rhp,nhp->rhn', query_flattened, key_flat, precision=HIGHEST)
        point_distance = lax.optimization_barrier(jnp.sum(jnp.square(query_flattened), -1))[:, :, None] + key_square[None] - 2.0 * cross_term
        pair_float = pair_rows.astype(jnp.float32)
        pair_head_bias = rounded(jnp.einsum('rjc,ch->rhj', pair_float, head_bias_weight.astype(jnp.float32), precision=HIGHEST))
        within_chain = (chain_rows[:, None] == residue_chain_index[None, :]).astype(jnp.float32)
        logit_matrix = LOGIT_FACTOR * (scalar_logit_term / math.sqrt(HEAD_FEATURES) + pair_head_bias.astype(jnp.float32) + chain_logit_offset[None, :, None] * within_chain[:, None, :] - (0.5 * point_term_weight * head_distance_weight)[None, :, None] * point_distance)
        logit_matrix = jnp.where(key_present[None, None, :], logit_matrix, -1000000000.0)
        weights = jax.nn.softmax(logit_matrix, axis=-1)
        attention = rounded(weights).astype(jnp.float32)
        scalar_out = jnp.einsum('rhn,nhc->rhc', attention, value_float, precision=HIGHEST)
        point_global = jnp.einsum('rhn,nhp->rhp', attention, value_flat, precision=HIGHEST).reshape(block_rows, HEAD_TOTAL, PV, 3)
        centred = point_global - trans_rows[:, None, None, :]
        point_local = lax.optimization_barrier(jnp.sum(rot_rows[:, None, None, :, :] * centred[:, :, :, :, None], axis=-2))
        point_norm = jnp.sqrt(lax.optimization_barrier(jnp.sum(jnp.square(point_local), -1)) + 1.0)
        pair_attended = jnp.einsum('rhj,rjc->rhc', attention, pair_float, precision=HIGHEST)
        features = jnp.concatenate([scalar_out, point_local.reshape(block_rows, HEAD_TOTAL, 3 * PV), point_norm], -1)
        first_part = jnp.einsum('rhf,hfd->rd', features, local_output_weight.astype(jnp.float32), precision=HIGHEST)
        second_part = jnp.einsum('rhc,hcd->rd', pair_attended, pair_output_weight.astype(jnp.float32), precision=HIGHEST)
        return first_part + second_part
    update = lax.map(attend, (query_values.reshape(block_count, block_rows, HEAD_TOTAL, HEAD_FEATURES), query_points.reshape(block_count, block_rows, HEAD_TOTAL, PQ, 3), pair.reshape(block_count, block_rows, RESIDUES, C_Z), rot_cols.reshape(block_count, block_rows, 3, 3), trans_cols.reshape(block_count, block_rows, 3), residue_chain_index.reshape(block_count, block_rows))).reshape(RESIDUES, D)
    single_out = rounded(layer_norm(single.astype(jnp.float32) + update, single_norm_gain))
    live_all = (residue_move_mask > 0).astype(jnp.float32)
    step_ratio = 1.0 / (STEPS - timestep[0]).astype(jnp.float32)
    rot_out, trans_out = frame_step(single_out, frame_velocity_weight, rot_cols, trans_cols, live_all, step_ratio)
    left_proj = rounded(jnp.dot(single_out, left_pair_weight, preferred_element_type=jnp.float32))
    right_float = rounded(jnp.dot(single_out, right_pair_weight, preferred_element_type=jnp.float32)).astype(jnp.float32)
    pair_block = math.gcd(RESIDUES, 32)
    pair_count = RESIDUES // pair_block

    def transition(args):
        pair_rows, left_rows, live_rows = args
        summed = pair_rows.astype(jnp.float32) + left_rows.astype(jnp.float32)[:, None, :] + right_float[None]
        normed = rounded(layer_norm(summed, pair_norm_gain)).astype(jnp.float32)
        hidden_one = rounded(jax.nn.relu(jnp.einsum('rjc,ck->rjk', normed, transition_hidden_weight.astype(jnp.float32), precision=HIGHEST))).astype(jnp.float32)
        hidden_two = rounded(jax.nn.relu(jnp.einsum('rjc,ck->rjk', hidden_one, transition_middle_weight.astype(jnp.float32), precision=HIGHEST))).astype(jnp.float32)
        branch = jnp.einsum('rjk,kc->rjc', hidden_two, transition_back_weight.astype(jnp.float32), precision=HIGHEST)
        pair_live = (live_rows[:, None] * live_all[None, :])[:, :, None]
        return rounded(pair_rows.astype(jnp.float32) + pair_live * branch)
    pair_out = lax.map(transition, (pair.reshape(pair_count, pair_block, RESIDUES, C_Z), left_proj.reshape(pair_count, pair_block, C_Z), live_all.reshape(pair_count, pair_block))).reshape(RESIDUES, RESIDUES, C_Z)
    return (single_out, rot_out, trans_out, pair_out)
```

```python
import math

import jax
import jax.numpy as jnp
from jax import lax
from jax.experimental import pallas as pl
from jax.experimental.pallas import tpu as pltpu
from jax.sharding import PartitionSpec as P

HEAD_FEATURES = 16
PQ = 8
PV = 12
STEPS = 8


LOGIT_FACTOR = math.sqrt(1.0 / 3.0)
HIGHEST = lax.Precision.HIGHEST


def rounded(values):
    return lax.optimization_barrier(values.astype(jnp.bfloat16))


def layer_norm(values, gain):
    centre = jnp.mean(values, axis=-1, keepdims=True)
    variance = jnp.mean(jnp.square(values - centre), axis=-1, keepdims=True)
    return (values - centre) * lax.rsqrt(variance + 1e-05) * gain


def to_global(local, rot_cols, trans_cols, npoints):
    rows_here = local.shape[0]
    heads_here = local.shape[1]
    points = local.reshape(rows_here, heads_here, npoints, 3)
    turned = jnp.sum(rot_cols[:, None, None, :, :] * points[:, :, :, None, :], axis=-1)
    return turned + trans_cols[:, None, None, :]


def key_features(projected, rot_cols, trans_cols):
    rows_here = projected.shape[0]
    heads_here = projected.shape[1]
    offset = 3 * HEAD_FEATURES
    key_points = to_global(
        projected[:, :, offset + 3 * PQ : offset + 6 * PQ], rot_cols, trans_cols, PQ
    )
    value_points = to_global(projected[:, :, offset + 6 * PQ :], rot_cols, trans_cols, PV)
    packed_projection = jnp.concatenate(
        [
            projected[:, :, HEAD_FEATURES : 3 * HEAD_FEATURES],
            key_points.reshape(rows_here, heads_here, 3 * PQ),
            value_points.reshape(rows_here, heads_here, 3 * PV),
        ],
        axis=-1,
    )
    return rounded(
        packed_projection.reshape(rows_here, heads_here * (2 * HEAD_FEATURES + 3 * PQ + 3 * PV))
    )


def hat_matrix(vectors):
    comp_x = vectors[:, 0]
    comp_y = vectors[:, 1]
    comp_z = vectors[:, 2]
    zeros_col = jnp.zeros_like(comp_x)
    first_row = jnp.stack([zeros_col, -comp_z, comp_y], -1)
    second_row = jnp.stack([comp_z, zeros_col, -comp_x], -1)
    third_row = jnp.stack([-comp_y, comp_x, zeros_col], -1)
    return jnp.stack([first_row, second_row, third_row], 1)


def frame_step(single_out, frame_velocity_weight, rot_cols, trans_cols, live_rows, step_ratio):
    motion = jnp.dot(single_out, frame_velocity_weight, preferred_element_type=jnp.float32)
    rotvec = step_ratio * jnp.tanh(motion[:, 0:3]) * live_rows[:, None]
    velocity = step_ratio * motion[:, 3:6] * live_rows[:, None]
    angle_sq = jnp.sum(jnp.square(rotvec), -1)
    coef_a = jnp.zeros_like(angle_sq)
    coef_b = jnp.zeros_like(angle_sq)
    coef_c = jnp.zeros_like(angle_sq)
    powers = jnp.ones_like(angle_sq)
    for order in range(8):
        parity = (-1.0) ** order
        coef_a = coef_a + powers * (parity / float(math.factorial(2 * order + 1)))
        coef_b = coef_b + powers * (parity / float(math.factorial(2 * order + 2)))
        coef_c = coef_c + powers * (parity / float(math.factorial(2 * order + 3)))
        powers = powers * angle_sq
    cross_mat = hat_matrix(rotvec)
    cross_sq = jnp.einsum("nab,nbc->nac", cross_mat, cross_mat, precision=HIGHEST)
    identity = jnp.eye(3, dtype=jnp.float32)[None]
    turn = identity + coef_a[:, None, None] * cross_mat + coef_b[:, None, None] * cross_sq
    jacobian = identity + coef_b[:, None, None] * cross_mat + coef_c[:, None, None] * cross_sq
    new_rot = jnp.einsum("nab,nbc->nac", rot_cols, turn, precision=HIGHEST)
    moved = jnp.einsum("nab,nb->na", jacobian, velocity, precision=HIGHEST)
    new_trans = trans_cols + jnp.einsum("nab,nb->na", rot_cols, moved, precision=HIGHEST)
    return (jnp.transpose(new_rot, (1, 2, 0)), jnp.transpose(new_trans))


def local_logit_rows(
    query_values,
    query_flattened,
    packed_projection,
    pair_head_bias,
    within_chain,
    distance_weight,
    chain_offset,
    key_present,
):
    key_scalar = packed_projection[:, :, 0:HEAD_FEATURES]
    key_flat = packed_projection[:, :, 2 * HEAD_FEATURES : 2 * HEAD_FEATURES + 3 * PQ].astype(
        jnp.float32
    )
    scalar_logit_term = jnp.einsum(
        "rhc,nhc->rhn", query_values, key_scalar, preferred_element_type=jnp.float32
    )
    cross_term = jnp.einsum("rhp,nhp->rhn", query_flattened, key_flat, precision=HIGHEST)
    key_square = jnp.transpose(jnp.sum(jnp.square(key_flat), -1))
    point_distance = (
        jnp.sum(jnp.square(query_flattened), -1)[:, :, None] + key_square[None] - 2.0 * cross_term
    )
    point_term_weight = math.sqrt(2.0 / (9.0 * PQ))
    logit_matrix = LOGIT_FACTOR * (
        scalar_logit_term / math.sqrt(HEAD_FEATURES)
        + pair_head_bias
        + chain_offset[None, :, None] * within_chain[:, None, :]
        - (0.5 * point_term_weight * distance_weight)[None, :, None] * point_distance
    )
    return jnp.where(key_present[None, None, :], logit_matrix, -1000000000.0)


def local_points(scalar_out, point_global, rot_own, trans_own, local_output_weight):
    rows_dev = scalar_out.shape[0]
    heads_here = scalar_out.shape[1]
    point_global = point_global.reshape(rows_dev, heads_here, PV, 3)
    centred = point_global - trans_own[:, None, None, :]
    point_local = jnp.sum(rot_own[:, None, None, :, :] * centred[:, :, :, :, None], axis=-2)
    point_norm = jnp.sqrt(jnp.sum(jnp.square(point_local), -1) + 1.0)
    features = jnp.concatenate(
        [scalar_out, point_local.reshape(rows_dev, heads_here, 3 * PV), point_norm], -1
    )
    return jnp.einsum(
        "rhf,hfd->rd", features, local_output_weight.astype(jnp.float32), precision=HIGHEST
    )


def push_blocks(src, buf, send_a, recv_a, send_b, recv_b):
    count = buf.shape[0]
    pairs = count // 2
    me = lax.axis_index("res")
    side = lax.rem(me, 2)
    chip = me // 2
    partner = chip * 2 + 1 - side

    def outgoing(step):
        target = partner if step == 0 else lax.rem(chip + step, pairs) * 2 + side
        return pltpu.make_async_remote_copy(
            src_ref=src,
            dst_ref=buf.at[me],
            send_sem=send_a.at[step],
            recv_sem=recv_a.at[step],
            device_id={"res": target},
            device_id_type=pl.DeviceIdType.MESH,
        )

    def passed_on(step):
        origin = lax.rem(chip + pairs - step, pairs) * 2 + side
        return pltpu.make_async_remote_copy(
            src_ref=buf.at[origin],
            dst_ref=buf.at[origin],
            send_sem=send_b.at[step],
            recv_sem=recv_b.at[step],
            device_id={"res": partner},
            device_id_type=pl.DeviceIdType.MESH,
        )

    def start():
        for step in range(1, pairs):
            outgoing(step).start()
        outgoing(0).start()
        buf[me] = src[...]

    def finish():
        for step in range(1, pairs):
            outgoing(step).wait_recv()
            passed_on(step).start()
        outgoing(0).wait_recv()
        for step in range(1, pairs):
            passed_on(step).wait_recv()
        for step in range(pairs):
            outgoing(step).wait_send()
        for step in range(1, pairs):
            passed_on(step).wait_send()

    return start, finish


def greet(count):
    pairs = count // 2
    me = lax.axis_index("res")
    side = lax.rem(me, 2)
    chip = me // 2
    barrier = pltpu.get_barrier_semaphore()
    for step in range(pairs):
        target = chip * 2 + 1 - side if step == 0 else lax.rem(chip + step, pairs) * 2 + side
        pl.semaphore_signal(
            barrier, inc=1, device_id={"res": target}, device_id_type=pl.DeviceIdType.MESH
        )
    pl.semaphore_wait(barrier, pairs)


def gather_kernel(src, out, buf, send_a, recv_a, send_b, recv_b):
    greet(buf.shape[0])
    start, finish = push_blocks(src, buf, send_a, recv_a, send_b, recv_b)
    start()
    finish()
    out[...] = buf[...]


def gather_blocks(block, count, collective_id):
    pairs = count // 2
    return pl.pallas_call(
        gather_kernel,
        out_shape=jax.ShapeDtypeStruct((count,) + block.shape, block.dtype),
        in_specs=[pl.BlockSpec(memory_space=pltpu.VMEM)],
        out_specs=pl.BlockSpec(memory_space=pltpu.VMEM),
        scratch_shapes=[pltpu.VMEM((count,) + block.shape, block.dtype)]
        + [pltpu.SemaphoreType.DMA((pairs,))] * 4,
        compiler_params=pltpu.CompilerParams(collective_id=collective_id, has_side_effects=True),
        name="gather_blocks",
    )(block)


def transition_kernel(
    live_rows, pair, left, right, live_cols, gain, first, middle, back, *rest
):
    *rest, wide = rest
    out = rest[len(rest) // 2]
    block = pair.shape[0]
    step = pl.program_id(0)
    own_start = lax.axis_index("res") * left.shape[0]

    @pl.when(step == 0)
    def _():
        live = jnp.where(live_cols[...] > 0, 1.0, 0.0)[None]
        wide[...] = jnp.transpose(jnp.broadcast_to(live, (wide.shape[1], wide.shape[0])))
        for src, dst in zip(rest[: len(rest) // 2], rest[len(rest) // 2 + 1 :]):
            dst[...] = src[...]

    cols, channels = pair.shape[1:]
    group = math.gcd(block, STACK)
    for row in range(0, block, group):
        stack = []
        for i in range(row, row + group):
            own = pair[i].astype(jnp.float32)
            summed = own + left[pl.ds(step * block + i, 1), :] + right[...]
            stack.append(layer_norm(summed, gain[...][None]).astype(jnp.bfloat16))
        normed = jnp.concatenate(stack, axis=0)
        hidden = jnp.dot(normed, first[...], preferred_element_type=jnp.float32)
        hidden = jnp.maximum(hidden.astype(jnp.bfloat16), 0)
        hidden = jnp.dot(hidden, middle[...], preferred_element_type=jnp.float32)
        hidden = jnp.maximum(hidden.astype(jnp.bfloat16), 0)
        branch = jnp.dot(hidden, back[...], preferred_element_type=jnp.float32)
        for i in range(row, row + group):
            live = jnp.where(live_rows[own_start + step * block + i] > 0, 1.0, 0.0)
            part = branch[(i - row) * cols : (i - row + 1) * cols]
            out[i] = (pair[i].astype(jnp.float32) + (live * wide[...]) * part).astype(jnp.bfloat16)


def run_transition(live_rows, pair, left, right, live_cols, gain, first, middle, back, *passed):
    rows, cols, channels = pair.shape
    block = math.gcd(rows, 12)
    whole = lambda a: pl.BlockSpec(a.shape, lambda i: (0,) * a.ndim)
    blocked = pl.BlockSpec((block, cols, channels), lambda i: (i, 0, 0))
    result = pl.pallas_call(
        transition_kernel,
        grid=(rows // block,),
        out_shape=[jax.ShapeDtypeStruct(a.shape, a.dtype) for a in (pair,) + passed],
        in_specs=[pl.BlockSpec(memory_space=pltpu.SMEM), blocked]
        + [whole(a) for a in (left, right, live_cols, gain, first, middle, back) + passed],
        out_specs=[blocked] + [whole(a) for a in passed],
        scratch_shapes=[pltpu.VMEM((cols, channels), jnp.float32)],
        name="transition",
    )(live_rows, pair, left, right, live_cols, gain, first, middle, back, *passed)
    return tuple(result[1:]) + (result[0],)


ROWS = 88
STACK = 4
PARTS = 2
PIECES = 1
GROUP = 4
FEAT = 80
NT = (((1,), (1,)), ((), ()))


def dot_nt(a, b):
    return lax.dot_general(a, b, NT, preferred_element_type=jnp.float32)


def lanes(ref, start, size, stride=1):
    at = pl.ds(start, size) if stride == 1 else pl.ds(start, size, stride)
    return jnp.concatenate([ref[c, at, :] for c in range(ref.shape[0])], axis=1)


def in_three(values):
    first = values.astype(jnp.bfloat16)
    rest = values - first.astype(jnp.float32)
    second = rest.astype(jnp.bfloat16)
    third = (rest - second.astype(jnp.float32)).astype(jnp.bfloat16)
    return first, second, third


def exact_dot(values, weight):
    rows = values.shape[0]
    stacked = jnp.concatenate(in_three(values), axis=0)
    result = jnp.dot(stacked, weight, preferred_element_type=jnp.float32)
    return result[2 * rows :] + result[rows : 2 * rows] + result[0:rows]


def flipped(chip, step):
    out, bit = chip, 1
    while bit <= step:
        if step & bit:
            out = out + bit * (1 - 2 * lax.rem(chip // bit, 2))
        bit *= 2
    return out


def position():
    me = lax.axis_index("res")
    return me, me // 2, lax.rem(me, 2)


def greet_all(count):
    me, chip, side = position()
    barrier = pltpu.get_barrier_semaphore()
    for step in reversed(range(count // 2)):
        for other in (0, 1):
            if step or other:
                target = flipped(chip, step) * 2 + (1 - side if other else side)
                pl.semaphore_signal(
                    barrier, inc=1, device_id={"res": target}, device_id_type=pl.DeviceIdType.MESH
                )
    return lambda: pl.semaphore_wait(barrier, count - 1)


def send_to(src, dst, send_sem, recv_sem, target):
    return pltpu.make_async_remote_copy(
        src_ref=src,
        dst_ref=dst,
        send_sem=send_sem,
        recv_sem=recv_sem,
        device_id={"res": target},
        device_id_type=pl.DeviceIdType.MESH,
    )


def gather_singles(src, buf, send_a, recv_a, send_b, recv_b):
    pairs = buf.shape[0] // 2
    me, chip, side = position()
    partner = chip * 2 + 1 - side

    def outgoing(step):
        target = flipped(chip, step) * 2 + side if step else partner
        return send_to(src, buf.at[me], send_a.at[step], recv_a.at[step], target)

    def passed_on(step):
        origin = flipped(chip, step) * 2 + side
        return send_to(buf.at[origin], buf.at[origin], send_b.at[step], recv_b.at[step], partner)

    def start():
        for step in reversed(range(pairs)):
            outgoing(step).start()
        buf[me] = src[...]

    def relay(step):
        outgoing(step).wait_recv()
        passed_on(step).start()

    def finish():
        outgoing(0).wait_recv()
        for step in range(1, pairs):
            passed_on(step).wait_recv()

    def drain():
        for step in range(pairs):
            outgoing(step).wait_send()
        for step in range(1, pairs):
            passed_on(step).wait_send()

    return start, relay, finish, drain


def share_block(src, buf, send, recv):
    pairs = buf.shape[0] // 2
    me, chip, side = position()

    def outgoing(step, other):
        target = flipped(chip, step) * 2 + (1 - side if other else side)
        at = 2 * step + other
        return send_to(src, buf.at[me], send.at[at], recv.at[at], target)

    everyone = [(step, other) for step in range(pairs) for other in (0, 1) if step or other]

    def start():
        for step, other in reversed(everyone):
            outgoing(step, other).start()
        buf[me] = src[...]

    def arrived(step):
        for other in (0, 1):
            if step or other:
                outgoing(step, other).wait_recv()

    def drain():
        for step, other in everyone:
            outgoing(step, other).wait_send()

    return start, arrived, drain


def turned_planes(planes, frame, transpose=False):
    out = []
    for a in range(3):
        rows = [3 * b + a if transpose else 3 * a + b for b in range(3)]
        out.append(
            frame[rows[0] : rows[0] + 1] * planes[0]
            + frame[rows[1] : rows[1] + 1] * planes[1]
            + frame[rows[2] : rows[2] + 1] * planes[2]
        )
    return out


OPERANDS = (
    "distance_weight",
    "chain_offset",
    "timestep",
    "single",
    "rotations",
    "translations",
    "chain",
    "mask",
    "bias_weight",
    "norm_gain",
    "velocity_weight",
    "left_weight",
    "right_weight",
    "proj",
    "pair",
    "local",
    "attended",
    "pair_gain",
    "first",
    "middle",
    "back",
)
SCALARS = 2


def step_kernel(*refs):
    count = len(OPERANDS)
    sources, refs = refs[:count], refs[count:]
    (single_out, rot_out, trans_out, pair_out), refs = refs[:4], refs[4:]
    held, refs = refs[:count], refs[count:]
    (
        buf,
        right_buf,
        right_own,
        frames,
        proj_all,
        proj_own,
        query_t,
        point_t,
        placed_t,
        squares,
        bias,
        attn,
        local_wide,
        local_planes,
        features,
        pair_rows,
        left_rows,
        row_gain,
        live_wide,
        centred_pair,
        normed,
        sems,
        send_a,
        recv_a,
        send_b,
        recv_b,
        send_c,
        recv_c,
    ) = refs
    (
        distance_weight,
        chain_offset,
        timestep,
        single,
        rotations,
        translations,
        chain,
        mask,
        bias_weight,
        norm_gain,
        velocity_weight,
        left_weight,
        right_weight,
        proj,
        pair,
        local,
        attended,
        pair_gain,
        first,
        middle,
        back,
    ) = held
    rows = single.shape[0]
    members = buf.shape[0]
    total = members * rows
    heads = bias_weight.shape[0]
    chunks = total // 128
    width = single.shape[1]
    shift = lax.rem(total - lax.axis_index("res") * rows, total)

    greeted = greet_all(members)
    loads = {
        name: pltpu.make_async_copy(src, dst, sems.at[i])
        for i, (name, src, dst) in enumerate(zip(OPERANDS, sources, held))
    }
    order = ["single"] + [name for name in OPERANDS if name != "single"]
    for name in order:
        loads[name].start()
    loads["single"].wait()
    greeted()
    start, relay, finish, drain = gather_singles(single, buf, send_a, recv_a, send_b, recv_b)
    start()

    for name in OPERANDS[: OPERANDS.index("proj")]:
        if name != "single":
            loads[name].wait()
    for a in range(3):
        frames[3 * a : 3 * a + 3, :] = rotations[a]
    frames[9:12, :] = translations[...]
    frames[12:13, :] = chain[...].astype(jnp.float32)[None]
    frames[13:14, :] = jnp.where(mask[...] > 0, 1.0, 0.0)[None]
    frames[14:16, :] = jnp.zeros((2, total), jnp.float32)
    own_wide = pltpu.roll(frames[...], shift, 1)[:, 0:128]
    own = own_wide[:, 0:rows]
    own_cols = jnp.transpose(own_wide)[0:rows]
    within = jnp.where(own_cols[:, 12:13] == frames[12:13, :], 1.0, 0.0)
    present = jnp.broadcast_to(frames[13:14, :], (rows, total)) > 0

    loads["proj"].wait()
    proj_own[:, 0:rows] = dot_nt(proj[...], single[...])
    for h in range(heads):
        query_t[h * 16 : h * 16 + 16, :] = proj_own[pl.ds(h, 16, heads), :]
    for p in range(PQ):
        planes = [
            proj_own[(48 + 3 * p + c) * heads : (49 + 3 * p + c) * heads, :] for c in range(3)
        ]
        for c, plane in enumerate(turned_planes(planes, own_wide)):
            point_t[pl.ds(3 * p + c, heads, 3 * PQ), :] = plane + own_wide[9 + c : 10 + c]
    queries = jnp.transpose(query_t[...])[0:rows].astype(jnp.bfloat16)
    points = jnp.transpose(point_t[...])[0:rows]
    point_parts = in_three(points)
    for c in range(chunks):
        for at in (36, 52, 68):
            for i in range(4):
                placed_t[c, pl.ds(at + i, heads, ROWS), :] = jnp.zeros((heads, 128), jnp.float32)

    loads["pair"].wait()
    bias_t = bias_weight[...]
    for r in range(rows):
        row = dot_nt(bias_t, pair[r]).astype(jnp.bfloat16).astype(jnp.float32)
        for c in range(chunks):
            bias[c, r * heads : (r + 1) * heads, :] = row[:, c * 128 : (c + 1) * 128]

    loads["local"].wait()
    for c in range(width // 128):
        local_wide[c, 0 : heads * 64, :] = local[:, c * 128 : (c + 1) * 128].astype(jnp.float32)
        local_wide[c, heads * 64 : heads * 64 + 8, :] = jnp.zeros((8, 128), jnp.float32)
    keep = lax.broadcasted_iota(jnp.int32, (16, width), 0) < PV
    for h in range(heads):
        base, at = h * 64, h * FEAT
        local_planes[at : at + 16, :] = local[base : base + 16, :]
        for c in range(3):
            plane = lanes(local_wide, base + 16 + c, 16, 3)
            local_planes[at + 16 * (c + 1) : at + 16 * (c + 2), :] = jnp.where(
                keep, plane, 0.0
            ).astype(jnp.bfloat16)
        plane = lanes(local_wide, base + 52, 16)
        local_planes[at + 64 : at + 80, :] = jnp.where(keep, plane, 0.0).astype(jnp.bfloat16)
    for name in OPERANDS[OPERANDS.index("attended") :]:
        loads[name].wait()
    live_wide[...] = jnp.transpose(
        jnp.broadcast_to(frames[13:14, :], (live_wide.shape[1], live_wide.shape[0]))
    )
    channels = pair.shape[2]
    row_gain[...] = own_cols[:, 13:14] * (math.sqrt(channels) * pair_gain[...])[None]

    pairs = members // 2
    for step in range(1, pairs):
        for i in range(rows * (step - 1) // (pairs - 1), rows * step // (pairs - 1)):
            own_pair = pair[i].astype(jnp.float32)
            centred_pair[i] = own_pair - jnp.mean(own_pair, axis=-1, keepdims=True)
        relay(step)
    finish()
    every = buf[...].astype(jnp.float32).reshape(total, width).astype(jnp.bfloat16)
    for c in range(chunks):
        proj_all[c] = dot_nt(proj[...], every[c * 128 : (c + 1) * 128])

    frame = frames[...]
    key_square = jnp.zeros((heads, total), jnp.float32)
    for p in range(PQ + PV):
        at = 72 + 3 * p
        planes = [lanes(proj_all, (at + c) * heads, heads) for c in range(3)]
        for c, plane in enumerate(turned_planes(planes, frame)):
            plane = (plane + frame[9 + c : 10 + c]).astype(jnp.bfloat16).astype(jnp.float32)
            if p < PQ:
                key_square = key_square + plane * plane
                slot = 3 * p + c
            else:
                slot = 24 + 16 * c + p - PQ
            for k in range(chunks):
                placed_t[k, pl.ds(slot, heads, ROWS), :] = plane[:, k * 128 : (k + 1) * 128]
    squares[...] = key_square

    for group in range(0, heads, GROUP):
        members_here = range(group, group + GROUP)
        logits = []
        for h in members_here:
            base = h * ROWS
            keys = lanes(proj_all, 16 * heads + h, 16, heads).astype(jnp.bfloat16)
            key_points = lanes(placed_t, base, 24).astype(jnp.bfloat16)
            query_points = points[:, h * 24 : h * 24 + 24]
            query_square = jnp.sum(query_points * query_points, axis=1, keepdims=True)
            stacked = jnp.concatenate(
                [part[:, h * 24 : h * 24 + 24] for part in point_parts], axis=0
            )
            cross = jnp.dot(stacked, key_points, preferred_element_type=jnp.float32)
            cross = cross[2 * rows : 3 * rows] + cross[rows : 2 * rows] + cross[0:rows]
            distance = query_square + squares[h : h + 1, :] - 2.0 * cross
            scalar = jnp.dot(
                queries[:, h * 16 : h * 16 + 16], keys, preferred_element_type=jnp.float32
            )
            logit = LOGIT_FACTOR * (
                scalar * (1.0 / math.sqrt(HEAD_FEATURES))
                + lanes(bias, h, rows, heads)
                + chain_offset[h] * within
                - (0.5 * math.sqrt(2.0 / (9.0 * PQ)) * distance_weight[h]) * distance
            )
            logits.append(jnp.where(present, logit, -1000000000.0))
        peaks = [jnp.max(logit, axis=1, keepdims=True) for logit in logits]
        exponents = [jnp.exp(logit - peak) for logit, peak in zip(logits, peaks)]
        sums = [jnp.sum(exponent, axis=1, keepdims=True) for exponent in exponents]
        attended_by = [
            (exponent / amount).astype(jnp.bfloat16) for exponent, amount in zip(exponents, sums)
        ]
        for h, weights in zip(members_here, attended_by):
            wide = weights.astype(jnp.float32)
            for c in range(chunks):
                attn[c, pl.ds(h, rows, heads), :] = wide[:, c * 128 : (c + 1) * 128]
        results = []
        for h, weights in zip(members_here, attended_by):
            values = lanes(proj_all, 32 * heads + h, 16, heads)
            stack = jnp.concatenate([values, lanes(placed_t, h * ROWS + 24, 48)], axis=0)
            results.append(dot_nt(stack.astype(jnp.bfloat16), weights))
        for h, result in zip(members_here, results):
            at = h * FEAT
            features[at : at + 16, 0:rows] = result[0:16]
            centred = [
                result[16 * (c + 1) : 16 * (c + 2)] - own[9 + c : 10 + c] for c in range(3)
            ]
            placed = turned_planes(centred, own, transpose=True)
            square = placed[0] * placed[0] + placed[1] * placed[1] + placed[2] * placed[2]
            for c in range(3):
                features[at + 16 * (c + 1) : at + 16 * (c + 2), 0:rows] = placed[c]
            features[at + 64 : at + 80, 0:rows] = jnp.sqrt(square + 1.0)

    for r in range(rows):
        weights = lanes(attn, r * heads, heads).astype(jnp.bfloat16)
        pair_rows[r * heads : (r + 1) * heads, :] = jnp.dot(
            weights, pair[r], preferred_element_type=jnp.float32
        )
    update = exact_dot(jnp.transpose(features[...])[0:rows], local_planes[...])
    attended_rows = jnp.concatenate(
        [pair_rows[pl.ds(h, rows, heads), :] for h in range(heads)], axis=1
    )
    update = update + exact_dot(attended_rows, attended[...])
    updated = layer_norm(single[...].astype(jnp.float32) + update, norm_gain[...][None])
    updated = updated.astype(jnp.bfloat16)
    right_own[...] = jnp.dot(
        updated, right_weight[...], preferred_element_type=jnp.float32
    ).astype(jnp.bfloat16)
    share, arrived, settle = share_block(right_own, right_buf, send_c, recv_c)
    share()
    single_out[...] = updated
    left = jnp.dot(updated, left_weight[...], preferred_element_type=jnp.float32)
    left = left.astype(jnp.bfloat16).astype(jnp.float32)
    left_rows[...] = left - jnp.mean(left, axis=-1, keepdims=True)

    motion = dot_nt(velocity_weight[...], updated)
    ratio = 1.0 / (STEPS - timestep[...]).astype(jnp.float32)
    live = own[13:14]
    turn_vec = ratio * jnp.tanh(motion[0:3]) * live
    speed = ratio * motion[3:6] * live
    x, y, z = turn_vec[0:1], turn_vec[1:2], turn_vec[2:3]
    angle = x * x + y * y + z * z
    coefs = [jnp.zeros_like(angle)] * 3
    powers = jnp.ones_like(angle)
    for order in range(8):
        parity = (-1.0) ** order
        coefs = [
            coef + powers * (parity / float(math.factorial(2 * order + 1 + i)))
            for i, coef in enumerate(coefs)
        ]
        powers = powers * angle
    zero = jnp.zeros_like(angle)
    cross_mat = [[zero, -z, y], [z, zero, -x], [-y, x, zero]]
    times = lambda p, q: [
        [sum(p[a][b] * q[b][c] for b in range(3)) for c in range(len(q[0]))] for a in range(3)
    ]
    squared = times(cross_mat, cross_mat)
    mix = lambda first, second: [
        [
            (1.0 if a == b else 0.0) + first * cross_mat[a][b] + second * squared[a][b]
            for b in range(3)
        ]
        for a in range(3)
    ]
    turn = mix(coefs[0], coefs[1])
    jacobian = mix(coefs[1], coefs[2])
    own_rot = [[own[3 * a + b : 3 * a + b + 1] for b in range(3)] for a in range(3)]
    new_rot = times(own_rot, turn)
    moved = times(own_rot, times(jacobian, [[speed[a : a + 1]] for a in range(3)]))
    for a in range(3):
        for b in range(3):
            rot_out[a, b : b + 1, :] = new_rot[a][b]
        trans_out[a : a + 1, :] = own[9 + a : 10 + a] + moved[a][0]
    drain()

    chip = position()[1]
    span = 2 * rows

    def columns(step):
        return pl.ds(pl.multiple_of(flipped(chip, step) * span, span), span)

    def prepare(step):
        at = columns(step)
        q = flipped(chip, step)
        arrived(step)
        right = jnp.concatenate([right_buf[2 * q], right_buf[2 * q + 1]], axis=0)
        right = right.astype(jnp.float32)
        right = right - jnp.mean(right, axis=-1, keepdims=True)
        live = live_wide[at, :]
        for i in range(rows):
            centred = centred_pair[i, at, :] + (left_rows[i : i + 1, :] + right)
            spread = jnp.sum(centred * centred, axis=-1, keepdims=True) + channels * 1e-05
            scaled = centred * (lax.rsqrt(spread) * live) * row_gain[i : i + 1, :]
            normed[step % 2, i * span : (i + 1) * span, :] = scaled.astype(jnp.bfloat16)

    def apply(step):
        at = columns(step)
        part = rows // PARTS
        for top in range(0, rows, part):
            hidden = normed[step % 2, top * span : (top + part) * span, :]
            hidden = jnp.dot(hidden, first[...], preferred_element_type=jnp.float32)
            hidden = jnp.maximum(hidden.astype(jnp.bfloat16), 0)
            hidden = jnp.dot(hidden, middle[...], preferred_element_type=jnp.float32)
            hidden = jnp.maximum(hidden.astype(jnp.bfloat16), 0)
            branch = jnp.dot(hidden, back[...], preferred_element_type=jnp.float32)
            for i in range(top, top + part):
                added = branch[(i - top) * span : (i - top + 1) * span]
                own_pair = pair[i, at, :].astype(jnp.float32)
                pair_out[i, at, :] = (own_pair + added).astype(jnp.bfloat16)

    steps = members // 2
    prepare(0)
    for step in range(steps):
        if step + 1 < steps:
            prepare(step + 1)
        apply(step)
    settle()


def deliver_kernel(*refs):
    *refs, sems = refs
    half = len(refs) // 2
    parts = []
    for src, dst in zip(refs[:half], refs[half:]):
        rows = src.shape[0]
        piece = rows // PIECES if len(src.shape) == 3 and rows % PIECES == 0 else rows
        for top in range(0, rows, piece):
            parts.append((src.at[pl.ds(top, piece)], dst.at[pl.ds(top, piece)]))
    copies = [
        pltpu.make_async_copy(src, dst, sems.at[i]) for i, (src, dst) in enumerate(parts)
    ]
    for copy in reversed(copies):
        copy.start()
    for copy in copies:
        copy.wait()


def deliver(*arrays):
    return pl.pallas_call(
        deliver_kernel,
        out_shape=[jax.ShapeDtypeStruct(a.shape, a.dtype) for a in arrays],
        in_specs=[pl.BlockSpec(memory_space=pltpu.VMEM)] * len(arrays),
        out_specs=[pl.BlockSpec(memory_space=pl.ANY)] * len(arrays),
        scratch_shapes=[pltpu.SemaphoreType.DMA((len(arrays) * PIECES,))],
        name="deliver",
    )(*[pltpu.with_memory_space_constraint(a, pltpu.VMEM) for a in arrays])


def run_step(
    single,
    pair,
    rotations,
    translations,
    chain,
    mask,
    timestep,
    proj,
    bias_weight,
    distance_weight,
    chain_offset,
    local,
    attended,
    norm_gain,
    velocity_weight,
    left_weight,
    right_weight,
    pair_gain,
    first,
    middle,
    back,
):
    rows, width = single.shape
    total = rotations.shape[2]
    members = total // rows
    pairs = members // 2
    heads = proj.shape[1]
    channels = pair.shape[2]
    chunks = total // 128
    proj_t = jnp.transpose(proj, (2, 1, 0)).reshape(-1, width)
    operands = dict(
        timestep=timestep.reshape(1, 1),
        distance_weight=distance_weight,
        chain_offset=chain_offset,
        single=single,
        rotations=rotations,
        translations=translations,
        chain=chain,
        mask=mask,
        bias_weight=jnp.transpose(bias_weight),
        norm_gain=norm_gain,
        velocity_weight=jnp.transpose(velocity_weight),
        left_weight=left_weight,
        right_weight=right_weight,
        proj=proj_t,
        pair=pair,
        local=local.reshape(-1, width),
        attended=attended.reshape(-1, width),
        pair_gain=pair_gain,
        first=first,
        middle=middle,
        back=back,
    )
    operands = [operands[name] for name in OPERANDS]
    bf16, f32 = jnp.bfloat16, jnp.float32
    scratch = [
        ((members, rows, width), bf16),
        ((members, rows, channels), bf16),
        ((rows, channels), bf16),
        ((16, total), f32),
        ((chunks, proj_t.shape[0], 128), f32),
        ((proj_t.shape[0], 128), f32),
        ((heads * 16, 128), f32),
        ((heads * 3 * PQ, 128), f32),
        ((chunks, heads * ROWS, 128), f32),
        ((heads, total), f32),
        ((chunks, rows * heads, total // chunks), f32),
        ((chunks, rows * heads, total // chunks), f32),
        ((width // 128, heads * 64 + 8, 128), f32),
        ((heads * FEAT, width), bf16),
        ((heads * FEAT, 128), f32),
        ((rows * heads, channels), f32),
        ((rows, channels), f32),
        ((rows, channels), f32),
        ((total, channels), f32),
        (pair.shape, f32),
        ((2, 2 * rows * rows, channels), bf16),
    ]
    dma = pltpu.SemaphoreType.DMA
    results = pl.pallas_call(
        step_kernel,
        out_shape=(
            pltpu.VMEM((rows, width), bf16),
            pltpu.VMEM((3, 3, rows), f32),
            pltpu.VMEM((3, rows), f32),
            pltpu.VMEM(pair.shape, bf16),
        ),
        in_specs=[pl.BlockSpec(memory_space=pl.ANY)] * len(operands),
        out_specs=(pl.BlockSpec(memory_space=pltpu.VMEM),) * 4,
        scratch_shapes=[pltpu.SMEM(a.shape, a.dtype) for a in operands[:SCALARS]]
        + [pltpu.VMEM(a.shape, a.dtype) for a in operands[SCALARS:]]
        + [pltpu.VMEM(*item) for item in scratch]
        + [dma((len(operands),))]
        + [dma((pairs,))] * 4
        + [dma((members,))] * 2,
        compiler_params=pltpu.CompilerParams(collective_id=2, has_side_effects=True),
        name="step",
    )(*operands)
    return deliver(*results)


def shards(
    single,
    pair,
    rotations,
    translations,
    residue_chain_index,
    residue_move_mask,
    timestep,
    single_projection_weight,
    head_bias_weight,
    head_distance_weight,
    chain_logit_offset,
    local_output_weight,
    pair_output_weight,
    single_norm_gain,
    frame_velocity_weight,
    left_pair_weight,
    right_pair_weight,
    pair_norm_gain,
    transition_hidden_weight,
    transition_middle_weight,
    transition_back_weight,
):
    rows_dev = single.shape[0]
    col_count = pair.shape[1]
    total = rotations.shape[2]
    heads_here = single_projection_weight.shape[1]
    row_start = lax.axis_index("res") * rows_dev
    col_start = lax.axis_index("head") * col_count
    pairs = total // rows_dev // 2
    if col_count == total and pairs & (pairs - 1) == 0 and rows_dev % 8 == 0:
        return tuple(
            run_step(
                single,
                pair,
                rotations,
                translations,
                residue_chain_index,
                residue_move_mask,
                timestep,
                single_projection_weight,
                head_bias_weight,
                head_distance_weight,
                chain_logit_offset,
                local_output_weight,
                pair_output_weight,
                single_norm_gain,
                frame_velocity_weight,
                left_pair_weight,
                right_pair_weight,
                pair_norm_gain,
                transition_hidden_weight,
                transition_middle_weight,
                transition_back_weight,
            )
        )
    rot_all = jnp.transpose(rotations, (2, 0, 1))
    trans_all = jnp.transpose(translations)
    rot_own = lax.dynamic_slice_in_dim(rot_all, row_start, rows_dev, 0)
    trans_own = lax.dynamic_slice_in_dim(trans_all, row_start, rows_dev, 0)
    own_chain = lax.dynamic_slice_in_dim(residue_chain_index, row_start, rows_dev, 0)
    offset = 3 * HEAD_FEATURES
    feat_count = 2 * HEAD_FEATURES + 3 * PQ + 3 * PV
    members = total // rows_dev
    every_single = gather_blocks(single, members, 0).reshape(total, -1)
    every_proj = jnp.einsum(
        "nd,dhf->nhf", every_single, single_projection_weight, preferred_element_type=jnp.float32
    )
    projected = lax.dynamic_slice_in_dim(every_proj, row_start, rows_dev, 0)
    packed_projection = key_features(every_proj, rot_all, trans_all)
    packed_projection = packed_projection.reshape(total, heads_here, feat_count)
    query_values = projected[:, :, 0:HEAD_FEATURES].astype(jnp.bfloat16)
    query_flattened = to_global(
        projected[:, :, offset : offset + 3 * PQ], rot_own, trans_own, PQ
    ).reshape(rows_dev, heads_here, 3 * PQ)
    bias_local = jnp.einsum(
        "rjc,ch->rhj", pair, head_bias_weight, preferred_element_type=jnp.float32
    ).astype(jnp.bfloat16)
    pair_head_bias = lax.all_to_all(
        bias_local, "head", split_axis=1, concat_axis=2, tiled=True
    ).astype(jnp.float32)
    within_chain = (own_chain[:, None] == residue_chain_index[None, :]).astype(jnp.float32)
    logit_matrix = local_logit_rows(
        query_values,
        query_flattened,
        packed_projection,
        pair_head_bias,
        within_chain,
        head_distance_weight,
        chain_logit_offset,
        residue_move_mask > 0,
    )
    peak = jnp.max(logit_matrix, axis=-1, keepdims=True)
    exponent = jnp.exp(logit_matrix - peak)
    attention = rounded(exponent / jnp.sum(exponent, axis=-1, keepdims=True))
    scalar_out = jnp.einsum(
        "rhn,nhc->rhc",
        attention,
        packed_projection[:, :, HEAD_FEATURES : 2 * HEAD_FEATURES],
        preferred_element_type=jnp.float32,
    )
    point_global = jnp.einsum(
        "rhn,nhp->rhp",
        attention.astype(jnp.float32),
        packed_projection[:, :, 2 * HEAD_FEATURES + 3 * PQ :].astype(jnp.float32),
        precision=HIGHEST,
    )
    update_local = local_points(scalar_out, point_global, rot_own, trans_own, local_output_weight)
    attention_cols = lax.all_to_all(attention, "head", split_axis=2, concat_axis=1, tiled=True)
    pair_attended = jnp.einsum(
        "rhj,rjc->rhc", attention_cols, pair, preferred_element_type=jnp.float32
    )
    update_pair = jnp.einsum(
        "rhc,hcd->rd", pair_attended, pair_output_weight.astype(jnp.float32), precision=HIGHEST
    )
    update = lax.psum(update_local + update_pair, "head")
    single_out = layer_norm(single.astype(jnp.float32) + update, single_norm_gain).astype(
        jnp.bfloat16
    )
    live_all = (residue_move_mask > 0).astype(jnp.float32)
    live_own = lax.dynamic_slice_in_dim(live_all, row_start, rows_dev, 0)
    step_ratio = 1.0 / (STEPS - timestep[0]).astype(jnp.float32)
    rot_out, trans_out = frame_step(
        single_out, frame_velocity_weight, rot_own, trans_own, live_own, step_ratio
    )
    left_proj = jnp.dot(single_out, left_pair_weight, preferred_element_type=jnp.float32).astype(
        jnp.bfloat16
    )
    own_right = jnp.dot(single_out, right_pair_weight, preferred_element_type=jnp.float32).astype(
        jnp.bfloat16
    )
    every_right = gather_blocks(own_right, members, 1).reshape(total, -1)
    right_proj = lax.dynamic_slice_in_dim(every_right, col_start, col_count, 0)
    (pair_out,) = run_transition(
        residue_move_mask,
        pair,
        left_proj.astype(jnp.float32),
        right_proj.astype(jnp.float32),
        lax.dynamic_slice_in_dim(residue_move_mask, col_start, col_count, 0),
        pair_norm_gain,
        transition_hidden_weight,
        transition_middle_weight,
        transition_back_weight,
    )
    return (single_out, rot_out, trans_out, pair_out)


def solution(mesh):
    placed = (
        P(("batch", "res"), None),
        P(("batch", "res"), "head", None),
        P(None, None, "batch"),
        P(None, "batch"),
        P(),
        P("batch"),
        P(),
        P(None, "head", None),
        P(),
        P("head"),
        P("head"),
        P("head", None, None),
        P(),
        P(),
        P(),
        P(),
        P(),
        P(),
        P(),
        P(),
        P(),
    )
    return jax.shard_map(
        shards,
        mesh=mesh,
        in_specs=placed,
        out_specs=(
            P(("batch", "res"), None),
            P(None, None, ("batch", "res")),
            P(None, ("batch", "res")),
            P(("batch", "res"), "head", None),
        ),
        check_vma=False,
    )
```

```python
import math

import jax
import jax.numpy as jnp
from jax import lax
from jax.experimental import pallas as pl
from jax.experimental.pallas import tpu as pltpu
from jax.sharding import PartitionSpec as P

HEAD_FEATURES = 16
PQ = 8
PV = 12
STEPS = 8


LOGIT_FACTOR = math.sqrt(1.0 / 3.0)
HIGHEST = lax.Precision.HIGHEST


def rounded(values):
    return lax.optimization_barrier(values.astype(jnp.bfloat16))


def layer_norm(values, gain):
    centre = jnp.mean(values, axis=-1, keepdims=True)
    variance = jnp.mean(jnp.square(values - centre), axis=-1, keepdims=True)
    return (values - centre) * lax.rsqrt(variance + 1e-05) * gain


def to_global(local, rot_cols, trans_cols, npoints):
    rows_here = local.shape[0]
    heads_here = local.shape[1]
    points = local.reshape(rows_here, heads_here, npoints, 3)
    turned = jnp.sum(rot_cols[:, None, None, :, :] * points[:, :, :, None, :], axis=-1)
    return turned + trans_cols[:, None, None, :]


def key_features(projected, rot_cols, trans_cols):
    rows_here = projected.shape[0]
    heads_here = projected.shape[1]
    offset = 3 * HEAD_FEATURES
    key_points = to_global(
        projected[:, :, offset + 3 * PQ : offset + 6 * PQ], rot_cols, trans_cols, PQ
    )
    value_points = to_global(projected[:, :, offset + 6 * PQ :], rot_cols, trans_cols, PV)
    packed_projection = jnp.concatenate(
        [
            projected[:, :, HEAD_FEATURES : 3 * HEAD_FEATURES],
            key_points.reshape(rows_here, heads_here, 3 * PQ),
            value_points.reshape(rows_here, heads_here, 3 * PV),
        ],
        axis=-1,
    )
    return rounded(
        packed_projection.reshape(rows_here, heads_here * (2 * HEAD_FEATURES + 3 * PQ + 3 * PV))
    )


def hat_matrix(vectors):
    comp_x = vectors[:, 0]
    comp_y = vectors[:, 1]
    comp_z = vectors[:, 2]
    zeros_col = jnp.zeros_like(comp_x)
    first_row = jnp.stack([zeros_col, -comp_z, comp_y], -1)
    second_row = jnp.stack([comp_z, zeros_col, -comp_x], -1)
    third_row = jnp.stack([-comp_y, comp_x, zeros_col], -1)
    return jnp.stack([first_row, second_row, third_row], 1)


def frame_step(single_out, frame_velocity_weight, rot_cols, trans_cols, live_rows, step_ratio):
    motion = jnp.dot(single_out, frame_velocity_weight, preferred_element_type=jnp.float32)
    rotvec = step_ratio * jnp.tanh(motion[:, 0:3]) * live_rows[:, None]
    velocity = step_ratio * motion[:, 3:6] * live_rows[:, None]
    angle_sq = jnp.sum(jnp.square(rotvec), -1)
    coef_a = jnp.zeros_like(angle_sq)
    coef_b = jnp.zeros_like(angle_sq)
    coef_c = jnp.zeros_like(angle_sq)
    powers = jnp.ones_like(angle_sq)
    for order in range(8):
        parity = (-1.0) ** order
        coef_a = coef_a + powers * (parity / float(math.factorial(2 * order + 1)))
        coef_b = coef_b + powers * (parity / float(math.factorial(2 * order + 2)))
        coef_c = coef_c + powers * (parity / float(math.factorial(2 * order + 3)))
        powers = powers * angle_sq
    cross_mat = hat_matrix(rotvec)
    cross_sq = jnp.einsum("nab,nbc->nac", cross_mat, cross_mat, precision=HIGHEST)
    identity = jnp.eye(3, dtype=jnp.float32)[None]
    turn = identity + coef_a[:, None, None] * cross_mat + coef_b[:, None, None] * cross_sq
    jacobian = identity + coef_b[:, None, None] * cross_mat + coef_c[:, None, None] * cross_sq
    new_rot = jnp.einsum("nab,nbc->nac", rot_cols, turn, precision=HIGHEST)
    moved = jnp.einsum("nab,nb->na", jacobian, velocity, precision=HIGHEST)
    new_trans = trans_cols + jnp.einsum("nab,nb->na", rot_cols, moved, precision=HIGHEST)
    return (jnp.transpose(new_rot, (1, 2, 0)), jnp.transpose(new_trans))


def local_logit_rows(
    query_values,
    query_flattened,
    packed_projection,
    pair_head_bias,
    within_chain,
    distance_weight,
    chain_offset,
    key_present,
):
    key_scalar = packed_projection[:, :, 0:HEAD_FEATURES]
    key_flat = packed_projection[:, :, 2 * HEAD_FEATURES : 2 * HEAD_FEATURES + 3 * PQ].astype(
        jnp.float32
    )
    scalar_logit_term = jnp.einsum(
        "rhc,nhc->rhn", query_values, key_scalar, preferred_element_type=jnp.float32
    )
    cross_term = jnp.einsum("rhp,nhp->rhn", query_flattened, key_flat, precision=HIGHEST)
    key_square = jnp.transpose(jnp.sum(jnp.square(key_flat), -1))
    point_distance = (
        jnp.sum(jnp.square(query_flattened), -1)[:, :, None] + key_square[None] - 2.0 * cross_term
    )
    point_term_weight = math.sqrt(2.0 / (9.0 * PQ))
    logit_matrix = LOGIT_FACTOR * (
        scalar_logit_term / math.sqrt(HEAD_FEATURES)
        + pair_head_bias
        + chain_offset[None, :, None] * within_chain[:, None, :]
        - (0.5 * point_term_weight * distance_weight)[None, :, None] * point_distance
    )
    return jnp.where(key_present[None, None, :], logit_matrix, -1000000000.0)


def local_points(scalar_out, point_global, rot_own, trans_own, local_output_weight):
    rows_dev = scalar_out.shape[0]
    heads_here = scalar_out.shape[1]
    point_global = point_global.reshape(rows_dev, heads_here, PV, 3)
    centred = point_global - trans_own[:, None, None, :]
    point_local = jnp.sum(rot_own[:, None, None, :, :] * centred[:, :, :, :, None], axis=-2)
    point_norm = jnp.sqrt(jnp.sum(jnp.square(point_local), -1) + 1.0)
    features = jnp.concatenate(
        [scalar_out, point_local.reshape(rows_dev, heads_here, 3 * PV), point_norm], -1
    )
    return jnp.einsum(
        "rhf,hfd->rd", features, local_output_weight.astype(jnp.float32), precision=HIGHEST
    )


def push_blocks(src, buf, send_a, recv_a, send_b, recv_b):
    count = buf.shape[0]
    pairs = count // 2
    me = lax.axis_index("res")
    side = lax.rem(me, 2)
    chip = me // 2
    partner = chip * 2 + 1 - side

    def outgoing(step):
        target = partner if step == 0 else lax.rem(chip + step, pairs) * 2 + side
        return pltpu.make_async_remote_copy(
            src_ref=src,
            dst_ref=buf.at[me],
            send_sem=send_a.at[step],
            recv_sem=recv_a.at[step],
            device_id={"res": target},
            device_id_type=pl.DeviceIdType.MESH,
        )

    def passed_on(step):
        origin = lax.rem(chip + pairs - step, pairs) * 2 + side
        return pltpu.make_async_remote_copy(
            src_ref=buf.at[origin],
            dst_ref=buf.at[origin],
            send_sem=send_b.at[step],
            recv_sem=recv_b.at[step],
            device_id={"res": partner},
            device_id_type=pl.DeviceIdType.MESH,
        )

    def start():
        for step in range(1, pairs):
            outgoing(step).start()
        outgoing(0).start()
        buf[me] = src[...]

    def finish():
        for step in range(1, pairs):
            outgoing(step).wait_recv()
            passed_on(step).start()
        outgoing(0).wait_recv()
        for step in range(1, pairs):
            passed_on(step).wait_recv()
        for step in range(pairs):
            outgoing(step).wait_send()
        for step in range(1, pairs):
            passed_on(step).wait_send()

    return start, finish


def greet(count):
    pairs = count // 2
    me = lax.axis_index("res")
    side = lax.rem(me, 2)
    chip = me // 2
    barrier = pltpu.get_barrier_semaphore()
    for step in range(pairs):
        target = chip * 2 + 1 - side if step == 0 else lax.rem(chip + step, pairs) * 2 + side
        pl.semaphore_signal(
            barrier, inc=1, device_id={"res": target}, device_id_type=pl.DeviceIdType.MESH
        )
    pl.semaphore_wait(barrier, pairs)


def gather_kernel(src, out, buf, send_a, recv_a, send_b, recv_b):
    greet(buf.shape[0])
    start, finish = push_blocks(src, buf, send_a, recv_a, send_b, recv_b)
    start()
    finish()
    out[...] = buf[...]


def gather_blocks(block, count, collective_id):
    pairs = count // 2
    return pl.pallas_call(
        gather_kernel,
        out_shape=jax.ShapeDtypeStruct((count,) + block.shape, block.dtype),
        in_specs=[pl.BlockSpec(memory_space=pltpu.VMEM)],
        out_specs=pl.BlockSpec(memory_space=pltpu.VMEM),
        scratch_shapes=[pltpu.VMEM((count,) + block.shape, block.dtype)]
        + [pltpu.SemaphoreType.DMA((pairs,))] * 4,
        compiler_params=pltpu.CompilerParams(collective_id=collective_id, has_side_effects=True),
        name="gather_blocks",
    )(block)


def transition_kernel(
    live_rows, pair, left, right, live_cols, gain, first, middle, back, *rest
):
    *rest, wide = rest
    out = rest[len(rest) // 2]
    block = pair.shape[0]
    step = pl.program_id(0)
    own_start = lax.axis_index("res") * left.shape[0]

    @pl.when(step == 0)
    def _():
        live = jnp.where(live_cols[...] > 0, 1.0, 0.0)[None]
        wide[...] = jnp.transpose(jnp.broadcast_to(live, (wide.shape[1], wide.shape[0])))
        for src, dst in zip(rest[: len(rest) // 2], rest[len(rest) // 2 + 1 :]):
            dst[...] = src[...]

    cols, channels = pair.shape[1:]
    group = math.gcd(block, STACK)
    for row in range(0, block, group):
        stack = []
        for i in range(row, row + group):
            own = pair[i].astype(jnp.float32)
            summed = own + left[pl.ds(step * block + i, 1), :] + right[...]
            stack.append(layer_norm(summed, gain[...][None]).astype(jnp.bfloat16))
        normed = jnp.concatenate(stack, axis=0)
        hidden = jnp.dot(normed, first[...], preferred_element_type=jnp.float32)
        hidden = jnp.maximum(hidden.astype(jnp.bfloat16), 0)
        hidden = jnp.dot(hidden, middle[...], preferred_element_type=jnp.float32)
        hidden = jnp.maximum(hidden.astype(jnp.bfloat16), 0)
        branch = jnp.dot(hidden, back[...], preferred_element_type=jnp.float32)
        for i in range(row, row + group):
            live = jnp.where(live_rows[own_start + step * block + i] > 0, 1.0, 0.0)
            part = branch[(i - row) * cols : (i - row + 1) * cols]
            out[i] = (pair[i].astype(jnp.float32) + (live * wide[...]) * part).astype(jnp.bfloat16)


def run_transition(live_rows, pair, left, right, live_cols, gain, first, middle, back, *passed):
    rows, cols, channels = pair.shape
    block = math.gcd(rows, 12)
    whole = lambda a: pl.BlockSpec(a.shape, lambda i: (0,) * a.ndim)
    blocked = pl.BlockSpec((block, cols, channels), lambda i: (i, 0, 0))
    result = pl.pallas_call(
        transition_kernel,
        grid=(rows // block,),
        out_shape=[jax.ShapeDtypeStruct(a.shape, a.dtype) for a in (pair,) + passed],
        in_specs=[pl.BlockSpec(memory_space=pltpu.SMEM), blocked]
        + [whole(a) for a in (left, right, live_cols, gain, first, middle, back) + passed],
        out_specs=[blocked] + [whole(a) for a in passed],
        scratch_shapes=[pltpu.VMEM((cols, channels), jnp.float32)],
        name="transition",
    )(live_rows, pair, left, right, live_cols, gain, first, middle, back, *passed)
    return tuple(result[1:]) + (result[0],)


ROWS = 88
STACK = 4
PARTS = 2
LATE = 2
GROUP = 4
FEAT = 80
NT = (((1,), (1,)), ((), ()))


def dot_nt(a, b):
    return lax.dot_general(a, b, NT, preferred_element_type=jnp.float32)


def lanes(ref, start, size, stride=1):
    at = pl.ds(start, size) if stride == 1 else pl.ds(start, size, stride)
    return jnp.concatenate([ref[c, at, :] for c in range(ref.shape[0])], axis=1)


def in_three(values):
    first = values.astype(jnp.bfloat16)
    rest = values - first.astype(jnp.float32)
    second = rest.astype(jnp.bfloat16)
    third = (rest - second.astype(jnp.float32)).astype(jnp.bfloat16)
    return first, second, third


def exact_dot(values, weight):
    rows = values.shape[0]
    stacked = jnp.concatenate(in_three(values), axis=0)
    result = jnp.dot(stacked, weight, preferred_element_type=jnp.float32)
    return result[2 * rows :] + result[rows : 2 * rows] + result[0:rows]


def flipped(chip, step):
    out, bit = chip, 1
    while bit <= step:
        if step & bit:
            out = out + bit * (1 - 2 * lax.rem(chip // bit, 2))
        bit *= 2
    return out


def chip_columns(chip, step, span):
    return pl.ds(pl.multiple_of(flipped(chip, step) * span, span), span)


def position():
    me = lax.axis_index("res")
    return me, me // 2, lax.rem(me, 2)


def greet_all(count):
    me, chip, side = position()
    barrier = pltpu.get_barrier_semaphore()
    for step in reversed(range(count // 2)):
        for other in (0, 1):
            if step or other:
                target = flipped(chip, step) * 2 + (1 - side if other else side)
                pl.semaphore_signal(
                    barrier, inc=1, device_id={"res": target}, device_id_type=pl.DeviceIdType.MESH
                )
    return lambda: pl.semaphore_wait(barrier, count - 1)


def send_to(src, dst, send_sem, recv_sem, target):
    return pltpu.make_async_remote_copy(
        src_ref=src,
        dst_ref=dst,
        send_sem=send_sem,
        recv_sem=recv_sem,
        device_id={"res": target},
        device_id_type=pl.DeviceIdType.MESH,
    )


def gather_singles(src, buf, send_a, recv_a, send_b, recv_b):
    pairs = buf.shape[0] // 2
    _, chip, side = position()
    partner = chip * 2 + 1 - side

    def outgoing(step):
        target = flipped(chip, step) * 2 + side if step else partner
        return send_to(src, buf.at[2 * step + side], send_a.at[step], recv_a.at[step], target)

    def passed_on(step):
        block = buf.at[2 * step + side]
        return send_to(block, block, send_b.at[step], recv_b.at[step], partner)

    def start():
        for step in reversed(range(pairs)):
            outgoing(step).start()
        buf[side] = src[...]

    def relay(step):
        outgoing(step).wait_recv()
        passed_on(step).start()

    def complete(step):
        if step:
            passed_on(step).wait_recv()
        else:
            outgoing(0).wait_recv()

    def drain():
        for step in range(pairs):
            outgoing(step).wait_send()
        for step in range(1, pairs):
            passed_on(step).wait_send()

    return start, relay, complete, drain


def share_block(src, buf, send, recv):
    pairs = buf.shape[0] // 2
    _, chip, side = position()

    def outgoing(step, other):
        target = flipped(chip, step) * 2 + (1 - side if other else side)
        at = 2 * step + other
        return send_to(src, buf.at[2 * step + side], send.at[at], recv.at[at], target)

    everyone = [(step, other) for step in range(pairs) for other in (0, 1) if step or other]

    def start():
        for step, other in everyone:
            outgoing(step, other).start()
        buf[side] = src[...]

    def arrived(step):
        for other in (0, 1):
            if step or other:
                outgoing(step, other).wait_recv()

    def drain():
        for step, other in everyone:
            outgoing(step, other).wait_send()

    return start, arrived, drain


def turned_planes(planes, frame, transpose=False):
    out = []
    for a in range(3):
        rows = [3 * b + a if transpose else 3 * a + b for b in range(3)]
        out.append(
            frame[rows[0] : rows[0] + 1] * planes[0]
            + frame[rows[1] : rows[1] + 1] * planes[1]
            + frame[rows[2] : rows[2] + 1] * planes[2]
        )
    return out


OPERANDS = (
    "distance_weight",
    "chain_offset",
    "timestep",
    "single",
    "rotations",
    "translations",
    "chain",
    "mask",
    "bias_weight",
    "norm_gain",
    "velocity_weight",
    "left_weight",
    "right_weight",
    "proj",
    "pair",
    "local",
    "attended",
    "pair_gain",
    "first",
    "middle",
    "back",
)
SCALARS = 2


def step_kernel(*refs):
    count = len(OPERANDS)
    sources, refs = refs[:count], refs[count:]
    single_out, rot_out, trans_out, pair_out, left_over, *weights_out = refs[:8]
    refs = refs[8:]
    held, refs = refs[: count - 3] + tuple(weights_out), refs[count - 3 :]
    (
        buf,
        right_buf,
        right_own,
        frames,
        frames_t,
        proj_all,
        proj_own,
        query_t,
        point_t,
        placed_t,
        squares,
        bias,
        attn,
        local_wide,
        local_planes,
        features,
        pair_rows,
        left_rows,
        row_gain,
        live_wide,
        centred_pair,
        normed,
        sems,
        pair_sems,
        send_a,
        recv_a,
        send_b,
        recv_b,
        send_c,
        recv_c,
    ) = refs
    (
        distance_weight,
        chain_offset,
        timestep,
        single,
        rotations,
        translations,
        chain,
        mask,
        bias_weight,
        norm_gain,
        velocity_weight,
        left_weight,
        right_weight,
        proj,
        pair,
        local,
        attended,
        pair_gain,
        first,
        middle,
        back,
    ) = held
    rows = single.shape[0]
    members = buf.shape[0]
    total = members * rows
    heads = bias_weight.shape[0]
    chunks = total // 128
    width = single.shape[1]
    pairs = members // 2
    span = 2 * rows
    me, chip, side = position()
    shift = lax.rem(total - side * rows, total)

    greeted = greet_all(members)
    loads = {
        name: pltpu.make_async_copy(src, dst, sems.at[i])
        for i, (name, src, dst) in enumerate(zip(OPERANDS, sources, held))
        if name != "pair"
    }
    loads["single"].start()
    for name, load in loads.items():
        if name != "single":
            load.start()
    pair_loads = [
        pltpu.make_async_copy(
            sources[OPERANDS.index("pair")].at[:, chip_columns(chip, step, span), :],
            pair.at[:, pl.ds(step * span, span), :],
            pair_sems.at[step],
        )
        for step in range(pairs)
    ]
    for load in pair_loads:
        load.start()
    loads["single"].wait()
    greeted()
    start, relay, complete, drain = gather_singles(single, buf, send_a, recv_a, send_b, recv_b)
    start()

    for name in OPERANDS[: OPERANDS.index("proj")]:
        if name != "single":
            loads[name].wait()
    for a in range(3):
        frames[3 * a : 3 * a + 3, :] = rotations[a]
    frames[9:12, :] = translations[...]
    frames[12:13, :] = chain[...].astype(jnp.float32)[None]
    frames[13:14, :] = jnp.where(mask[...] > 0, 1.0, 0.0)[None]
    frames[14:16, :] = jnp.zeros((2, total), jnp.float32)
    frames_t[...] = jnp.transpose(frames[...])
    own_cols = frames_t[pl.ds(pl.multiple_of(me * rows, rows), rows), :]
    near_t = jnp.concatenate(
        [frames_t[chip_columns(chip, step, span), :] for step in range(pairs)], axis=0
    )
    live_wide[...] = jnp.broadcast_to(near_t[:, 13:14], live_wide.shape)
    frame = jnp.transpose(near_t)
    frames[...] = frame
    own_wide = pltpu.roll(frame, shift, 1)[:, 0:128]
    own = own_wide[:, 0:rows]
    within = jnp.where(own_cols[:, 12:13] == frames[12:13, :], 1.0, 0.0)
    present = jnp.broadcast_to(frames[13:14, :], (rows, total)) > 0

    loads["proj"].wait()
    proj_own[:, 0:rows] = dot_nt(proj[...], single[...])
    for h in range(heads):
        query_t[h * 16 : h * 16 + 16, :] = proj_own[pl.ds(h, 16, heads), :]
    for p in range(PQ):
        planes = [
            proj_own[(48 + 3 * p + c) * heads : (49 + 3 * p + c) * heads, :] for c in range(3)
        ]
        for c, plane in enumerate(turned_planes(planes, own_wide)):
            point_t[pl.ds(3 * p + c, heads, 3 * PQ), :] = plane + own_wide[9 + c : 10 + c]
    queries = jnp.transpose(query_t[...])[0:rows].astype(jnp.bfloat16)
    points = jnp.transpose(point_t[...])[0:rows]
    point_parts = in_three(points)
    for c in range(chunks):
        for at in (36, 52, 68):
            for i in range(4):
                placed_t[c, pl.ds(at + i, heads, ROWS), :] = jnp.zeros((heads, 128), jnp.float32)

    for load in pair_loads:
        load.wait()
    bias_t = bias_weight[...]
    for r in range(rows):
        row = dot_nt(bias_t, pair[r]).astype(jnp.bfloat16).astype(jnp.float32)
        for c in range(chunks):
            bias[c, r * heads : (r + 1) * heads, :] = row[:, c * 128 : (c + 1) * 128]

    loads["local"].wait()
    for c in range(width // 128):
        local_wide[c, 0 : heads * 64, :] = local[:, c * 128 : (c + 1) * 128].astype(jnp.float32)
        local_wide[c, heads * 64 : heads * 64 + 8, :] = jnp.zeros((8, 128), jnp.float32)
    keep = lax.broadcasted_iota(jnp.int32, (16, width), 0) < PV
    for h in range(heads):
        base, at = h * 64, h * FEAT
        local_planes[at : at + 16, :] = local[base : base + 16, :]
        for c in range(3):
            plane = lanes(local_wide, base + 16 + c, 16, 3)
            local_planes[at + 16 * (c + 1) : at + 16 * (c + 2), :] = jnp.where(
                keep, plane, 0.0
            ).astype(jnp.bfloat16)
        plane = lanes(local_wide, base + 52, 16)
        local_planes[at + 64 : at + 80, :] = jnp.where(keep, plane, 0.0).astype(jnp.bfloat16)
    for name in OPERANDS[OPERANDS.index("attended") :]:
        loads[name].wait()
    channels = pair.shape[2]
    row_gain[...] = own_cols[:, 13:14] * (math.sqrt(channels) * pair_gain[...])[None]

    def centre(top, bottom):
        for i in range(top, bottom):
            own_pair = pair[i].astype(jnp.float32)
            centred_pair[i] = own_pair - jnp.mean(own_pair, axis=-1, keepdims=True)

    def project(c):
        lead = c * 128 // rows
        blocks = [buf[m].astype(jnp.float32) for m in range(lead, -(-(c + 1) * 128 // rows))]
        skip = c * 128 - lead * rows
        every = jnp.concatenate(blocks, axis=0)[skip : skip + 128]
        proj_all[c] = dot_nt(proj[...], every.astype(jnp.bfloat16))
        at_lanes = slice(c * 128, (c + 1) * 128)
        turn_here = frames[:, at_lanes]
        key_square = jnp.zeros((heads, 128), jnp.float32)
        for p in range(PQ + PV):
            at = 72 + 3 * p
            planes = [proj_all[c, (at + k) * heads : (at + k + 1) * heads, :] for k in range(3)]
            for k, plane in enumerate(turned_planes(planes, turn_here)):
                plane = plane + turn_here[9 + k : 10 + k]
                plane = plane.astype(jnp.bfloat16).astype(jnp.float32)
                if p < PQ:
                    key_square = key_square + plane * plane
                    slot = 3 * p + k
                else:
                    slot = 24 + 16 * k + p - PQ
                placed_t[c, pl.ds(slot, heads, ROWS), :] = plane
        squares[:, at_lanes] = key_square

    half = pairs // 2
    for step in range(1, half):
        relay(step)
    centre(0, rows)
    for step in range(half, pairs):
        relay(step)
    known = 0
    for c in range(chunks):
        need = min(pairs - 1, ((c + 1) * 128 - 1) // span)
        for step in range(known, need + 1):
            complete(step)
        known = need + 1
        project(c)

    for group in range(0, heads, GROUP):
        members_here = range(group, group + GROUP)
        logits = []
        for h in members_here:
            base = h * ROWS
            keys = lanes(proj_all, 16 * heads + h, 16, heads).astype(jnp.bfloat16)
            key_points = lanes(placed_t, base, 24).astype(jnp.bfloat16)
            query_points = points[:, h * 24 : h * 24 + 24]
            query_square = jnp.sum(query_points * query_points, axis=1, keepdims=True)
            stacked = jnp.concatenate(
                [part[:, h * 24 : h * 24 + 24] for part in point_parts], axis=0
            )
            cross = jnp.dot(stacked, key_points, preferred_element_type=jnp.float32)
            cross = cross[2 * rows : 3 * rows] + cross[rows : 2 * rows] + cross[0:rows]
            distance = query_square + squares[h : h + 1, :] - 2.0 * cross
            scalar = jnp.dot(
                queries[:, h * 16 : h * 16 + 16], keys, preferred_element_type=jnp.float32
            )
            logit = LOGIT_FACTOR * (
                scalar * (1.0 / math.sqrt(HEAD_FEATURES))
                + lanes(bias, h, rows, heads)
                + chain_offset[h] * within
                - (0.5 * math.sqrt(2.0 / (9.0 * PQ)) * distance_weight[h]) * distance
            )
            logits.append(jnp.where(present, logit, -1000000000.0))
        peaks = [jnp.max(logit, axis=1, keepdims=True) for logit in logits]
        exponents = [jnp.exp(logit - peak) for logit, peak in zip(logits, peaks)]
        sums = [jnp.sum(exponent, axis=1, keepdims=True) for exponent in exponents]
        attended_by = [
            (exponent / amount).astype(jnp.bfloat16) for exponent, amount in zip(exponents, sums)
        ]
        for h, weights in zip(members_here, attended_by):
            wide = weights.astype(jnp.float32)
            for c in range(chunks):
                attn[c, pl.ds(h, rows, heads), :] = wide[:, c * 128 : (c + 1) * 128]
        results = []
        for h, weights in zip(members_here, attended_by):
            values = lanes(proj_all, 32 * heads + h, 16, heads)
            stack = jnp.concatenate([values, lanes(placed_t, h * ROWS + 24, 48)], axis=0)
            results.append(dot_nt(stack.astype(jnp.bfloat16), weights))
        for h, result in zip(members_here, results):
            at = h * FEAT
            features[at : at + 16, 0:rows] = result[0:16]
            centred = [
                result[16 * (c + 1) : 16 * (c + 2)] - own[9 + c : 10 + c] for c in range(3)
            ]
            placed = turned_planes(centred, own, transpose=True)
            square = placed[0] * placed[0] + placed[1] * placed[1] + placed[2] * placed[2]
            for c in range(3):
                features[at + 16 * (c + 1) : at + 16 * (c + 2), 0:rows] = placed[c]
            features[at + 64 : at + 80, 0:rows] = jnp.sqrt(square + 1.0)

    for r in range(rows):
        weights = lanes(attn, r * heads, heads).astype(jnp.bfloat16)
        pair_rows[r * heads : (r + 1) * heads, :] = jnp.dot(
            weights, pair[r], preferred_element_type=jnp.float32
        )
    update = exact_dot(jnp.transpose(features[...])[0:rows], local_planes[...])
    attended_rows = jnp.concatenate(
        [pair_rows[pl.ds(h, rows, heads), :] for h in range(heads)], axis=1
    )
    update = update + exact_dot(attended_rows, attended[...])
    updated = layer_norm(single[...].astype(jnp.float32) + update, norm_gain[...][None])
    updated = updated.astype(jnp.bfloat16)
    right_own[...] = jnp.dot(
        updated, right_weight[...], preferred_element_type=jnp.float32
    ).astype(jnp.bfloat16)
    share, arrived, settle = share_block(right_own, right_buf, send_c, recv_c)
    share()
    single_out[...] = updated
    left = jnp.dot(updated, left_weight[...], preferred_element_type=jnp.float32)
    left = left.astype(jnp.bfloat16).astype(jnp.float32)
    left_rows[...] = left - jnp.mean(left, axis=-1, keepdims=True)

    motion = dot_nt(velocity_weight[...], updated)
    ratio = 1.0 / (STEPS - timestep[...]).astype(jnp.float32)
    live = own[13:14]
    turn_vec = ratio * jnp.tanh(motion[0:3]) * live
    speed = ratio * motion[3:6] * live
    x, y, z = turn_vec[0:1], turn_vec[1:2], turn_vec[2:3]
    angle = x * x + y * y + z * z
    coefs = [jnp.zeros_like(angle)] * 3
    powers = jnp.ones_like(angle)
    for order in range(8):
        parity = (-1.0) ** order
        coefs = [
            coef + powers * (parity / float(math.factorial(2 * order + 1 + i)))
            for i, coef in enumerate(coefs)
        ]
        powers = powers * angle
    zero = jnp.zeros_like(angle)
    cross_mat = [[zero, -z, y], [z, zero, -x], [-y, x, zero]]
    times = lambda p, q: [
        [sum(p[a][b] * q[b][c] for b in range(3)) for c in range(len(q[0]))] for a in range(3)
    ]
    squared = times(cross_mat, cross_mat)
    mix = lambda first, second: [
        [
            (1.0 if a == b else 0.0) + first * cross_mat[a][b] + second * squared[a][b]
            for b in range(3)
        ]
        for a in range(3)
    ]
    turn = mix(coefs[0], coefs[1])
    jacobian = mix(coefs[1], coefs[2])
    own_rot = [[own[3 * a + b : 3 * a + b + 1] for b in range(3)] for a in range(3)]
    new_rot = times(own_rot, turn)
    moved = times(own_rot, times(jacobian, [[speed[a : a + 1]] for a in range(3)]))
    for a in range(3):
        for b in range(3):
            rot_out[a, b : b + 1, :] = new_rot[a][b]
        trans_out[a : a + 1, :] = own[9 + a : 10 + a] + moved[a][0]
    drain()

    def prepare(step):
        at = pl.ds(step * span, span)
        arrived(step)
        right = jnp.concatenate([right_buf[2 * step], right_buf[2 * step + 1]], axis=0)
        right = right.astype(jnp.float32)
        right = right - jnp.mean(right, axis=-1, keepdims=True)
        live = live_wide[at, :]
        late = step - (pairs - LATE)
        into = normed.at[step % 2] if late < 0 else left_over.at[late]
        for i in range(rows):
            centred = centred_pair[i, at, :] + (left_rows[i : i + 1, :] + right)
            spread = jnp.sum(centred * centred, axis=-1, keepdims=True) + channels * 1e-05
            scaled = centred * (lax.rsqrt(spread) * live) * row_gain[i : i + 1, :]
            into[i * span : (i + 1) * span, :] = scaled.astype(jnp.bfloat16)
        if late >= 0:
            pair_out[:, at, :] = pair[:, at, :]

    prepare(0)
    for step in range(pairs - LATE):
        prepare(step + 1)
        if step + 1 == pairs - LATE:
            for late in range(step + 2, pairs):
                prepare(late)
        at = step * span
        add_branch(normed.at[step % 2], pair, pair_out, at, span, first, middle, back)
    settle()


def add_branch(normed, pair, out, at, span, first, middle, back, out_at=None):
    rows = pair.shape[0]
    part = rows // PARTS
    out_at = at if out_at is None else out_at
    for top in range(0, rows, part):
        hidden = normed[top * span : (top + part) * span, :]
        hidden = jnp.dot(hidden, first[...], preferred_element_type=jnp.float32)
        hidden = jnp.maximum(hidden.astype(jnp.bfloat16), 0)
        hidden = jnp.dot(hidden, middle[...], preferred_element_type=jnp.float32)
        hidden = jnp.maximum(hidden.astype(jnp.bfloat16), 0)
        branch = jnp.dot(hidden, back[...], preferred_element_type=jnp.float32)
        for i in range(top, top + part):
            added = branch[(i - top) * span : (i - top + 1) * span]
            own_pair = pair[i, pl.ds(at, span), :].astype(jnp.float32)
            out[i, pl.ds(out_at, span), :] = (own_pair + added).astype(jnp.bfloat16)


def deliver_kernel(
    single,
    rot,
    trans,
    pair,
    left_over,
    first,
    middle,
    back,
    single_out,
    rot_out,
    trans_out,
    pair_out,
    block,
    sems,
):
    _, chip, _ = position()
    span = 2 * pair.shape[0]
    pairs = pair.shape[1] // span

    def place(src, step):
        return pltpu.make_async_copy(
            src, pair_out.at[:, chip_columns(chip, step, span), :], sems.at[step]
        )

    copies = [place(pair.at[:, pl.ds(s * span, span), :], s) for s in range(pairs - LATE)]
    copies += [
        pltpu.make_async_copy(src, dst, sems.at[pairs + i])
        for i, (src, dst) in enumerate(
            [(single, single_out), (rot, rot_out), (trans, trans_out)]
        )
    ]
    for copy in copies:
        copy.start()
    for late in range(LATE):
        step = pairs - LATE + late
        into = block.at[late]
        add_branch(left_over.at[late], pair, into, step * span, span, first, middle, back, 0)
        last = place(into, step)
        last.start()
        copies.append(last)
    for copy in copies:
        copy.wait()


def deliver(*arrays):
    rows, cols, channels = arrays[3].shape
    pairs = cols // (2 * rows)
    return pl.pallas_call(
        deliver_kernel,
        out_shape=[jax.ShapeDtypeStruct(a.shape, a.dtype) for a in arrays[:4]],
        in_specs=[pl.BlockSpec(memory_space=pltpu.VMEM)] * len(arrays),
        out_specs=[pl.BlockSpec(memory_space=pl.ANY)] * 4,
        scratch_shapes=[
            pltpu.VMEM((LATE, rows, 2 * rows, channels), arrays[3].dtype),
            pltpu.SemaphoreType.DMA((pairs + 3,)),
        ],
        name="deliver",
    )(*[pltpu.with_memory_space_constraint(a, pltpu.VMEM) for a in arrays])


def run_step(
    single,
    pair,
    rotations,
    translations,
    chain,
    mask,
    timestep,
    proj,
    bias_weight,
    distance_weight,
    chain_offset,
    local,
    attended,
    norm_gain,
    velocity_weight,
    left_weight,
    right_weight,
    pair_gain,
    first,
    middle,
    back,
):
    rows, width = single.shape
    total = rotations.shape[2]
    members = total // rows
    pairs = members // 2
    heads = proj.shape[1]
    channels = pair.shape[2]
    chunks = total // 128
    proj_t = jnp.transpose(proj, (2, 1, 0)).reshape(-1, width)
    operands = dict(
        timestep=timestep.reshape(1, 1),
        distance_weight=distance_weight,
        chain_offset=chain_offset,
        single=single,
        rotations=rotations,
        translations=translations,
        chain=chain,
        mask=mask,
        bias_weight=jnp.transpose(bias_weight),
        norm_gain=norm_gain,
        velocity_weight=jnp.transpose(velocity_weight),
        left_weight=left_weight,
        right_weight=right_weight,
        proj=proj_t,
        pair=pair,
        local=local.reshape(-1, width),
        attended=attended.reshape(-1, width),
        pair_gain=pair_gain,
        first=first,
        middle=middle,
        back=back,
    )
    operands = [operands[name] for name in OPERANDS]
    bf16, f32 = jnp.bfloat16, jnp.float32
    scratch = [
        ((members, rows, width), bf16),
        ((members, rows, channels), bf16),
        ((rows, channels), bf16),
        ((16, total), f32),
        ((total, 16), f32),
        ((chunks, proj_t.shape[0], 128), f32),
        ((proj_t.shape[0], 128), f32),
        ((heads * 16, 128), f32),
        ((heads * 3 * PQ, 128), f32),
        ((chunks, heads * ROWS, 128), f32),
        ((heads, total), f32),
        ((chunks, rows * heads, total // chunks), f32),
        ((chunks, rows * heads, total // chunks), f32),
        ((width // 128, heads * 64 + 8, 128), f32),
        ((heads * FEAT, width), bf16),
        ((heads * FEAT, 128), f32),
        ((rows * heads, channels), f32),
        ((rows, channels), f32),
        ((rows, channels), f32),
        ((total, channels), f32),
        (pair.shape, f32),
        ((2, 2 * rows * rows, channels), bf16),
    ]
    dma = pltpu.SemaphoreType.DMA
    results = pl.pallas_call(
        step_kernel,
        out_shape=(
            pltpu.VMEM((rows, width), bf16),
            pltpu.VMEM((3, 3, rows), f32),
            pltpu.VMEM((3, rows), f32),
            pltpu.VMEM(pair.shape, bf16),
            pltpu.VMEM((LATE, 2 * rows * rows, channels), bf16),
            *[pltpu.VMEM(a.shape, a.dtype) for a in operands[-3:]],
        ),
        in_specs=[pl.BlockSpec(memory_space=pl.ANY)] * len(operands),
        out_specs=(pl.BlockSpec(memory_space=pltpu.VMEM),) * 8,
        scratch_shapes=[pltpu.SMEM(a.shape, a.dtype) for a in operands[:SCALARS]]
        + [pltpu.VMEM(a.shape, a.dtype) for a in operands[SCALARS:-3]]
        + [pltpu.VMEM(*item) for item in scratch]
        + [dma((len(operands),)), dma((pairs,))]
        + [dma((pairs,))] * 4
        + [dma((members,))] * 2,
        compiler_params=pltpu.CompilerParams(collective_id=2, has_side_effects=True),
        name="step",
    )(*operands)
    return deliver(*results)


def shards(
    single,
    pair,
    rotations,
    translations,
    residue_chain_index,
    residue_move_mask,
    timestep,
    single_projection_weight,
    head_bias_weight,
    head_distance_weight,
    chain_logit_offset,
    local_output_weight,
    pair_output_weight,
    single_norm_gain,
    frame_velocity_weight,
    left_pair_weight,
    right_pair_weight,
    pair_norm_gain,
    transition_hidden_weight,
    transition_middle_weight,
    transition_back_weight,
):
    rows_dev = single.shape[0]
    col_count = pair.shape[1]
    total = rotations.shape[2]
    heads_here = single_projection_weight.shape[1]
    row_start = lax.axis_index("res") * rows_dev
    col_start = lax.axis_index("head") * col_count
    pairs = total // rows_dev // 2
    if col_count == total and pairs & (pairs - 1) == 0 and pairs > LATE and rows_dev % 8 == 0:
        return tuple(
            run_step(
                single,
                pair,
                rotations,
                translations,
                residue_chain_index,
                residue_move_mask,
                timestep,
                single_projection_weight,
                head_bias_weight,
                head_distance_weight,
                chain_logit_offset,
                local_output_weight,
                pair_output_weight,
                single_norm_gain,
                frame_velocity_weight,
                left_pair_weight,
                right_pair_weight,
                pair_norm_gain,
                transition_hidden_weight,
                transition_middle_weight,
                transition_back_weight,
            )
        )
    rot_all = jnp.transpose(rotations, (2, 0, 1))
    trans_all = jnp.transpose(translations)
    rot_own = lax.dynamic_slice_in_dim(rot_all, row_start, rows_dev, 0)
    trans_own = lax.dynamic_slice_in_dim(trans_all, row_start, rows_dev, 0)
    own_chain = lax.dynamic_slice_in_dim(residue_chain_index, row_start, rows_dev, 0)
    offset = 3 * HEAD_FEATURES
    feat_count = 2 * HEAD_FEATURES + 3 * PQ + 3 * PV
    members = total // rows_dev
    every_single = gather_blocks(single, members, 0).reshape(total, -1)
    every_proj = jnp.einsum(
        "nd,dhf->nhf", every_single, single_projection_weight, preferred_element_type=jnp.float32
    )
    projected = lax.dynamic_slice_in_dim(every_proj, row_start, rows_dev, 0)
    packed_projection = key_features(every_proj, rot_all, trans_all)
    packed_projection = packed_projection.reshape(total, heads_here, feat_count)
    query_values = projected[:, :, 0:HEAD_FEATURES].astype(jnp.bfloat16)
    query_flattened = to_global(
        projected[:, :, offset : offset + 3 * PQ], rot_own, trans_own, PQ
    ).reshape(rows_dev, heads_here, 3 * PQ)
    bias_local = jnp.einsum(
        "rjc,ch->rhj", pair, head_bias_weight, preferred_element_type=jnp.float32
    ).astype(jnp.bfloat16)
    pair_head_bias = lax.all_to_all(
        bias_local, "head", split_axis=1, concat_axis=2, tiled=True
    ).astype(jnp.float32)
    within_chain = (own_chain[:, None] == residue_chain_index[None, :]).astype(jnp.float32)
    logit_matrix = local_logit_rows(
        query_values,
        query_flattened,
        packed_projection,
        pair_head_bias,
        within_chain,
        head_distance_weight,
        chain_logit_offset,
        residue_move_mask > 0,
    )
    peak = jnp.max(logit_matrix, axis=-1, keepdims=True)
    exponent = jnp.exp(logit_matrix - peak)
    attention = rounded(exponent / jnp.sum(exponent, axis=-1, keepdims=True))
    scalar_out = jnp.einsum(
        "rhn,nhc->rhc",
        attention,
        packed_projection[:, :, HEAD_FEATURES : 2 * HEAD_FEATURES],
        preferred_element_type=jnp.float32,
    )
    point_global = jnp.einsum(
        "rhn,nhp->rhp",
        attention.astype(jnp.float32),
        packed_projection[:, :, 2 * HEAD_FEATURES + 3 * PQ :].astype(jnp.float32),
        precision=HIGHEST,
    )
    update_local = local_points(scalar_out, point_global, rot_own, trans_own, local_output_weight)
    attention_cols = lax.all_to_all(attention, "head", split_axis=2, concat_axis=1, tiled=True)
    pair_attended = jnp.einsum(
        "rhj,rjc->rhc", attention_cols, pair, preferred_element_type=jnp.float32
    )
    update_pair = jnp.einsum(
        "rhc,hcd->rd", pair_attended, pair_output_weight.astype(jnp.float32), precision=HIGHEST
    )
    update = lax.psum(update_local + update_pair, "head")
    single_out = layer_norm(single.astype(jnp.float32) + update, single_norm_gain).astype(
        jnp.bfloat16
    )
    live_all = (residue_move_mask > 0).astype(jnp.float32)
    live_own = lax.dynamic_slice_in_dim(live_all, row_start, rows_dev, 0)
    step_ratio = 1.0 / (STEPS - timestep[0]).astype(jnp.float32)
    rot_out, trans_out = frame_step(
        single_out, frame_velocity_weight, rot_own, trans_own, live_own, step_ratio
    )
    left_proj = jnp.dot(single_out, left_pair_weight, preferred_element_type=jnp.float32).astype(
        jnp.bfloat16
    )
    own_right = jnp.dot(single_out, right_pair_weight, preferred_element_type=jnp.float32).astype(
        jnp.bfloat16
    )
    every_right = gather_blocks(own_right, members, 1).reshape(total, -1)
    right_proj = lax.dynamic_slice_in_dim(every_right, col_start, col_count, 0)
    (pair_out,) = run_transition(
        residue_move_mask,
        pair,
        left_proj.astype(jnp.float32),
        right_proj.astype(jnp.float32),
        lax.dynamic_slice_in_dim(residue_move_mask, col_start, col_count, 0),
        pair_norm_gain,
        transition_hidden_weight,
        transition_middle_weight,
        transition_back_weight,
    )
    return (single_out, rot_out, trans_out, pair_out)


def solution(mesh):
    placed = (
        P(("batch", "res"), None),
        P(("batch", "res"), "head", None),
        P(None, None, "batch"),
        P(None, "batch"),
        P(),
        P("batch"),
        P(),
        P(None, "head", None),
        P(),
        P("head"),
        P("head"),
        P("head", None, None),
        P(),
        P(),
        P(),
        P(),
        P(),
        P(),
        P(),
        P(),
        P(),
    )
    return jax.shard_map(
        shards,
        mesh=mesh,
        in_specs=placed,
        out_specs=(
            P(("batch", "res"), None),
            P(None, None, ("batch", "res")),
            P(None, ("batch", "res")),
            P(("batch", "res"), "head", None),
        ),
        check_vma=False,
    )
```

```python
import math

import jax
import jax.numpy as jnp
from jax import lax
from jax.experimental import pallas as pl
from jax.experimental.pallas import tpu as pltpu
from jax.sharding import PartitionSpec as P

HEAD_FEATURES = 16
PQ = 8
PV = 12
STEPS = 8


LOGIT_FACTOR = math.sqrt(1.0 / 3.0)
HIGHEST = lax.Precision.HIGHEST


def rounded(values):
    return lax.optimization_barrier(values.astype(jnp.bfloat16))


def layer_norm(values, gain):
    centre = jnp.mean(values, axis=-1, keepdims=True)
    variance = jnp.mean(jnp.square(values - centre), axis=-1, keepdims=True)
    return (values - centre) * lax.rsqrt(variance + 1e-05) * gain


def to_global(local, rot_cols, trans_cols, npoints):
    rows_here = local.shape[0]
    heads_here = local.shape[1]
    points = local.reshape(rows_here, heads_here, npoints, 3)
    turned = jnp.sum(rot_cols[:, None, None, :, :] * points[:, :, :, None, :], axis=-1)
    return turned + trans_cols[:, None, None, :]


def key_features(projected, rot_cols, trans_cols):
    rows_here = projected.shape[0]
    heads_here = projected.shape[1]
    offset = 3 * HEAD_FEATURES
    key_points = to_global(
        projected[:, :, offset + 3 * PQ : offset + 6 * PQ], rot_cols, trans_cols, PQ
    )
    value_points = to_global(projected[:, :, offset + 6 * PQ :], rot_cols, trans_cols, PV)
    packed_projection = jnp.concatenate(
        [
            projected[:, :, HEAD_FEATURES : 3 * HEAD_FEATURES],
            key_points.reshape(rows_here, heads_here, 3 * PQ),
            value_points.reshape(rows_here, heads_here, 3 * PV),
        ],
        axis=-1,
    )
    return rounded(
        packed_projection.reshape(rows_here, heads_here * (2 * HEAD_FEATURES + 3 * PQ + 3 * PV))
    )


def hat_matrix(vectors):
    comp_x = vectors[:, 0]
    comp_y = vectors[:, 1]
    comp_z = vectors[:, 2]
    zeros_col = jnp.zeros_like(comp_x)
    first_row = jnp.stack([zeros_col, -comp_z, comp_y], -1)
    second_row = jnp.stack([comp_z, zeros_col, -comp_x], -1)
    third_row = jnp.stack([-comp_y, comp_x, zeros_col], -1)
    return jnp.stack([first_row, second_row, third_row], 1)


def frame_step(single_out, frame_velocity_weight, rot_cols, trans_cols, live_rows, step_ratio):
    motion = jnp.dot(single_out, frame_velocity_weight, preferred_element_type=jnp.float32)
    rotvec = step_ratio * jnp.tanh(motion[:, 0:3]) * live_rows[:, None]
    velocity = step_ratio * motion[:, 3:6] * live_rows[:, None]
    angle_sq = jnp.sum(jnp.square(rotvec), -1)
    coef_a = jnp.zeros_like(angle_sq)
    coef_b = jnp.zeros_like(angle_sq)
    coef_c = jnp.zeros_like(angle_sq)
    powers = jnp.ones_like(angle_sq)
    for order in range(8):
        parity = (-1.0) ** order
        coef_a = coef_a + powers * (parity / float(math.factorial(2 * order + 1)))
        coef_b = coef_b + powers * (parity / float(math.factorial(2 * order + 2)))
        coef_c = coef_c + powers * (parity / float(math.factorial(2 * order + 3)))
        powers = powers * angle_sq
    cross_mat = hat_matrix(rotvec)
    cross_sq = jnp.einsum("nab,nbc->nac", cross_mat, cross_mat, precision=HIGHEST)
    identity = jnp.eye(3, dtype=jnp.float32)[None]
    turn = identity + coef_a[:, None, None] * cross_mat + coef_b[:, None, None] * cross_sq
    jacobian = identity + coef_b[:, None, None] * cross_mat + coef_c[:, None, None] * cross_sq
    new_rot = jnp.einsum("nab,nbc->nac", rot_cols, turn, precision=HIGHEST)
    moved = jnp.einsum("nab,nb->na", jacobian, velocity, precision=HIGHEST)
    new_trans = trans_cols + jnp.einsum("nab,nb->na", rot_cols, moved, precision=HIGHEST)
    return (jnp.transpose(new_rot, (1, 2, 0)), jnp.transpose(new_trans))


def local_logit_rows(
    query_values,
    query_flattened,
    packed_projection,
    pair_head_bias,
    within_chain,
    distance_weight,
    chain_offset,
    key_present,
):
    key_scalar = packed_projection[:, :, 0:HEAD_FEATURES]
    key_flat = packed_projection[:, :, 2 * HEAD_FEATURES : 2 * HEAD_FEATURES + 3 * PQ].astype(
        jnp.float32
    )
    scalar_logit_term = jnp.einsum(
        "rhc,nhc->rhn", query_values, key_scalar, preferred_element_type=jnp.float32
    )
    cross_term = jnp.einsum("rhp,nhp->rhn", query_flattened, key_flat, precision=HIGHEST)
    key_square = jnp.transpose(jnp.sum(jnp.square(key_flat), -1))
    point_distance = (
        jnp.sum(jnp.square(query_flattened), -1)[:, :, None] + key_square[None] - 2.0 * cross_term
    )
    point_term_weight = math.sqrt(2.0 / (9.0 * PQ))
    logit_matrix = LOGIT_FACTOR * (
        scalar_logit_term / math.sqrt(HEAD_FEATURES)
        + pair_head_bias
        + chain_offset[None, :, None] * within_chain[:, None, :]
        - (0.5 * point_term_weight * distance_weight)[None, :, None] * point_distance
    )
    return jnp.where(key_present[None, None, :], logit_matrix, -1000000000.0)


def local_points(scalar_out, point_global, rot_own, trans_own, local_output_weight):
    rows_dev = scalar_out.shape[0]
    heads_here = scalar_out.shape[1]
    point_global = point_global.reshape(rows_dev, heads_here, PV, 3)
    centred = point_global - trans_own[:, None, None, :]
    point_local = jnp.sum(rot_own[:, None, None, :, :] * centred[:, :, :, :, None], axis=-2)
    point_norm = jnp.sqrt(jnp.sum(jnp.square(point_local), -1) + 1.0)
    features = jnp.concatenate(
        [scalar_out, point_local.reshape(rows_dev, heads_here, 3 * PV), point_norm], -1
    )
    return jnp.einsum(
        "rhf,hfd->rd", features, local_output_weight.astype(jnp.float32), precision=HIGHEST
    )


def push_blocks(src, buf, send_a, recv_a, send_b, recv_b):
    count = buf.shape[0]
    pairs = count // 2
    me = lax.axis_index("res")
    side = lax.rem(me, 2)
    chip = me // 2
    partner = chip * 2 + 1 - side

    def outgoing(step):
        target = partner if step == 0 else lax.rem(chip + step, pairs) * 2 + side
        return pltpu.make_async_remote_copy(
            src_ref=src,
            dst_ref=buf.at[me],
            send_sem=send_a.at[step],
            recv_sem=recv_a.at[step],
            device_id={"res": target},
            device_id_type=pl.DeviceIdType.MESH,
        )

    def passed_on(step):
        origin = lax.rem(chip + pairs - step, pairs) * 2 + side
        return pltpu.make_async_remote_copy(
            src_ref=buf.at[origin],
            dst_ref=buf.at[origin],
            send_sem=send_b.at[step],
            recv_sem=recv_b.at[step],
            device_id={"res": partner},
            device_id_type=pl.DeviceIdType.MESH,
        )

    def start():
        for step in range(1, pairs):
            outgoing(step).start()
        outgoing(0).start()
        buf[me] = src[...]

    def finish():
        for step in range(1, pairs):
            outgoing(step).wait_recv()
            passed_on(step).start()
        outgoing(0).wait_recv()
        for step in range(1, pairs):
            passed_on(step).wait_recv()
        for step in range(pairs):
            outgoing(step).wait_send()
        for step in range(1, pairs):
            passed_on(step).wait_send()

    return start, finish


def greet(count):
    pairs = count // 2
    me = lax.axis_index("res")
    side = lax.rem(me, 2)
    chip = me // 2
    barrier = pltpu.get_barrier_semaphore()
    for step in range(pairs):
        target = chip * 2 + 1 - side if step == 0 else lax.rem(chip + step, pairs) * 2 + side
        pl.semaphore_signal(
            barrier, inc=1, device_id={"res": target}, device_id_type=pl.DeviceIdType.MESH
        )
    pl.semaphore_wait(barrier, pairs)


def gather_kernel(src, out, buf, send_a, recv_a, send_b, recv_b):
    greet(buf.shape[0])
    start, finish = push_blocks(src, buf, send_a, recv_a, send_b, recv_b)
    start()
    finish()
    out[...] = buf[...]


def gather_blocks(block, count, collective_id):
    pairs = count // 2
    return pl.pallas_call(
        gather_kernel,
        out_shape=jax.ShapeDtypeStruct((count,) + block.shape, block.dtype),
        in_specs=[pl.BlockSpec(memory_space=pltpu.VMEM)],
        out_specs=pl.BlockSpec(memory_space=pltpu.VMEM),
        scratch_shapes=[pltpu.VMEM((count,) + block.shape, block.dtype)]
        + [pltpu.SemaphoreType.DMA((pairs,))] * 4,
        compiler_params=pltpu.CompilerParams(collective_id=collective_id, has_side_effects=True),
        name="gather_blocks",
    )(block)


def transition_kernel(
    live_rows, pair, left, right, live_cols, gain, first, middle, back, *rest
):
    *rest, wide = rest
    out = rest[len(rest) // 2]
    block = pair.shape[0]
    step = pl.program_id(0)
    own_start = lax.axis_index("res") * left.shape[0]

    @pl.when(step == 0)
    def _():
        live = jnp.where(live_cols[...] > 0, 1.0, 0.0)[None]
        wide[...] = jnp.transpose(jnp.broadcast_to(live, (wide.shape[1], wide.shape[0])))
        for src, dst in zip(rest[: len(rest) // 2], rest[len(rest) // 2 + 1 :]):
            dst[...] = src[...]

    cols, channels = pair.shape[1:]
    group = math.gcd(block, STACK)
    for row in range(0, block, group):
        stack = []
        for i in range(row, row + group):
            own = pair[i].astype(jnp.float32)
            summed = own + left[pl.ds(step * block + i, 1), :] + right[...]
            stack.append(layer_norm(summed, gain[...][None]).astype(jnp.bfloat16))
        normed = jnp.concatenate(stack, axis=0)
        hidden = jnp.dot(normed, first[...], preferred_element_type=jnp.float32)
        hidden = jnp.maximum(hidden.astype(jnp.bfloat16), 0)
        hidden = jnp.dot(hidden, middle[...], preferred_element_type=jnp.float32)
        hidden = jnp.maximum(hidden.astype(jnp.bfloat16), 0)
        branch = jnp.dot(hidden, back[...], preferred_element_type=jnp.float32)
        for i in range(row, row + group):
            live = jnp.where(live_rows[own_start + step * block + i] > 0, 1.0, 0.0)
            part = branch[(i - row) * cols : (i - row + 1) * cols]
            out[i] = (pair[i].astype(jnp.float32) + (live * wide[...]) * part).astype(jnp.bfloat16)


def run_transition(live_rows, pair, left, right, live_cols, gain, first, middle, back, *passed):
    rows, cols, channels = pair.shape
    block = math.gcd(rows, 12)
    whole = lambda a: pl.BlockSpec(a.shape, lambda i: (0,) * a.ndim)
    blocked = pl.BlockSpec((block, cols, channels), lambda i: (i, 0, 0))
    result = pl.pallas_call(
        transition_kernel,
        grid=(rows // block,),
        out_shape=[jax.ShapeDtypeStruct(a.shape, a.dtype) for a in (pair,) + passed],
        in_specs=[pl.BlockSpec(memory_space=pltpu.SMEM), blocked]
        + [whole(a) for a in (left, right, live_cols, gain, first, middle, back) + passed],
        out_specs=[blocked] + [whole(a) for a in passed],
        scratch_shapes=[pltpu.VMEM((cols, channels), jnp.float32)],
        name="transition",
    )(live_rows, pair, left, right, live_cols, gain, first, middle, back, *passed)
    return tuple(result[1:]) + (result[0],)


ROWS = 88
STACK = 4
PARTS = 1
LATE = 2
GROUP = 16
FEAT = 80
NT = (((1,), (1,)), ((), ()))


def dot_nt(a, b):
    return lax.dot_general(a, b, NT, preferred_element_type=jnp.float32)


def lanes(ref, start, size, stride=1):
    at = pl.ds(start, size) if stride == 1 else pl.ds(start, size, stride)
    return jnp.concatenate([ref[c, at, :] for c in range(ref.shape[0])], axis=1)


def in_three(values):
    first = values.astype(jnp.bfloat16)
    rest = values - first.astype(jnp.float32)
    second = rest.astype(jnp.bfloat16)
    third = (rest - second.astype(jnp.float32)).astype(jnp.bfloat16)
    return first, second, third


def exact_dot(values, weight):
    rows = values.shape[0]
    stacked = jnp.concatenate(in_three(values), axis=0)
    result = jnp.dot(stacked, weight, preferred_element_type=jnp.float32)
    return result[2 * rows :] + result[rows : 2 * rows] + result[0:rows]


def flipped(chip, step):
    out, bit = chip, 1
    while bit <= step:
        if step & bit:
            out = out + bit * (1 - 2 * lax.rem(chip // bit, 2))
        bit *= 2
    return out


def chip_columns(chip, step, span):
    return pl.ds(pl.multiple_of(flipped(chip, step) * span, span), span)


def position():
    me = lax.axis_index("res")
    return me, me // 2, lax.rem(me, 2)


def greet_all(count):
    me, chip, side = position()
    barrier = pltpu.get_barrier_semaphore()
    for step in reversed(range(count // 2)):
        for other in (0, 1):
            if step or other:
                target = flipped(chip, step) * 2 + (1 - side if other else side)
                pl.semaphore_signal(
                    barrier, inc=1, device_id={"res": target}, device_id_type=pl.DeviceIdType.MESH
                )
    return lambda: pl.semaphore_wait(barrier, count - 1)


def send_to(src, dst, send_sem, recv_sem, target):
    return pltpu.make_async_remote_copy(
        src_ref=src,
        dst_ref=dst,
        send_sem=send_sem,
        recv_sem=recv_sem,
        device_id={"res": target},
        device_id_type=pl.DeviceIdType.MESH,
    )


def gather_singles(src, buf, send_a, recv_a, send_b, recv_b):
    pairs = buf.shape[0] // 2
    _, chip, side = position()
    partner = chip * 2 + 1 - side

    def outgoing(step):
        target = flipped(chip, step) * 2 + side if step else partner
        return send_to(src, buf.at[2 * step + side], send_a.at[step], recv_a.at[step], target)

    def passed_on(step):
        block = buf.at[2 * step + side]
        return send_to(block, block, send_b.at[step], recv_b.at[step], partner)

    def start():
        for step in reversed(range(pairs)):
            outgoing(step).start()
        buf[side] = src[...]

    def relay(step):
        outgoing(step).wait_recv()
        passed_on(step).start()

    def complete(step):
        if step:
            passed_on(step).wait_recv()
        else:
            outgoing(0).wait_recv()

    def drain():
        for step in range(pairs):
            outgoing(step).wait_send()
        for step in range(1, pairs):
            passed_on(step).wait_send()

    return start, relay, complete, drain


def share_block(src, buf, send, recv):
    pairs = buf.shape[0] // 2
    _, chip, side = position()

    def outgoing(step, other):
        target = flipped(chip, step) * 2 + (1 - side if other else side)
        at = 2 * step + other
        return send_to(src, buf.at[2 * step + side], send.at[at], recv.at[at], target)

    everyone = [(step, other) for step in range(pairs) for other in (0, 1) if step or other]

    def start():
        for step, other in everyone:
            outgoing(step, other).start()
        buf[side] = src[...]

    def arrived(step):
        for other in (0, 1):
            if step or other:
                outgoing(step, other).wait_recv()

    def drain():
        for step, other in everyone:
            outgoing(step, other).wait_send()

    return start, arrived, drain


def turned_planes(planes, frame, transpose=False):
    out = []
    for a in range(3):
        rows = [3 * b + a if transpose else 3 * a + b for b in range(3)]
        out.append(
            frame[rows[0] : rows[0] + 1] * planes[0]
            + frame[rows[1] : rows[1] + 1] * planes[1]
            + frame[rows[2] : rows[2] + 1] * planes[2]
        )
    return out


OPERANDS = (
    "distance_weight",
    "chain_offset",
    "timestep",
    "single",
    "rotations",
    "translations",
    "chain",
    "mask",
    "bias_weight",
    "norm_gain",
    "velocity_weight",
    "left_weight",
    "right_weight",
    "proj",
    "pair",
    "local",
    "attended",
    "pair_gain",
    "first",
    "middle",
    "back",
)
SCALARS = 2


def step_kernel(*refs):
    count = len(OPERANDS)
    sources, refs = refs[:count], refs[count:]
    single_out, rot_out, trans_out, pair_out, left_over, *weights_out = refs[:8]
    refs = refs[8:]
    held, refs = refs[: count - 3] + tuple(weights_out), refs[count - 3 :]
    (
        buf,
        right_buf,
        right_own,
        frames,
        frames_t,
        proj_all,
        proj_own,
        query_t,
        point_t,
        placed_t,
        squares,
        bias,
        attn,
        local_wide,
        local_planes,
        features,
        pair_rows,
        left_rows,
        row_gain,
        live_wide,
        centred_pair,
        normed,
        sems,
        pair_sems,
        send_a,
        recv_a,
        send_b,
        recv_b,
        send_c,
        recv_c,
    ) = refs
    (
        distance_weight,
        chain_offset,
        timestep,
        single,
        rotations,
        translations,
        chain,
        mask,
        bias_weight,
        norm_gain,
        velocity_weight,
        left_weight,
        right_weight,
        proj,
        pair,
        local,
        attended,
        pair_gain,
        first,
        middle,
        back,
    ) = held
    rows = single.shape[0]
    members = buf.shape[0]
    total = members * rows
    heads = bias_weight.shape[0]
    chunks = total // 128
    width = single.shape[1]
    pairs = members // 2
    span = 2 * rows
    me, chip, side = position()
    shift = lax.rem(total - side * rows, total)

    greeted = greet_all(members)
    loads = {
        name: pltpu.make_async_copy(src, dst, sems.at[i])
        for i, (name, src, dst) in enumerate(zip(OPERANDS, sources, held))
        if name != "pair"
    }
    loads["single"].start()
    for name, load in loads.items():
        if name != "single":
            load.start()
    pair_loads = [
        pltpu.make_async_copy(
            sources[OPERANDS.index("pair")].at[:, chip_columns(chip, step, span), :],
            pair.at[:, pl.ds(step * span, span), :],
            pair_sems.at[step],
        )
        for step in range(pairs)
    ]
    for load in pair_loads:
        load.start()
    loads["single"].wait()
    greeted()
    start, relay, complete, drain = gather_singles(single, buf, send_a, recv_a, send_b, recv_b)
    start()

    for name in OPERANDS[: OPERANDS.index("proj")]:
        if name != "single":
            loads[name].wait()
    for a in range(3):
        frames[3 * a : 3 * a + 3, :] = rotations[a]
    frames[9:12, :] = translations[...]
    frames[12:13, :] = chain[...].astype(jnp.float32)[None]
    frames[13:14, :] = jnp.where(mask[...] > 0, 1.0, 0.0)[None]
    frames[14:16, :] = jnp.zeros((2, total), jnp.float32)
    frames_t[...] = jnp.transpose(frames[...])
    own_cols = frames_t[pl.ds(pl.multiple_of(me * rows, rows), rows), :]
    near_t = jnp.concatenate(
        [frames_t[chip_columns(chip, step, span), :] for step in range(pairs)], axis=0
    )
    live_wide[...] = jnp.broadcast_to(near_t[:, 13:14], live_wide.shape)
    frame = jnp.transpose(near_t)
    frames[...] = frame
    own_wide = pltpu.roll(frame, shift, 1)[:, 0:128]
    own = own_wide[:, 0:rows]
    within = jnp.where(own_cols[:, 12:13] == frames[12:13, :], 1.0, 0.0)
    present = jnp.broadcast_to(frames[13:14, :], (rows, total)) > 0

    loads["proj"].wait()
    proj_own[:, 0:rows] = dot_nt(proj[...], single[...])
    for h in range(heads):
        query_t[h * 16 : h * 16 + 16, :] = proj_own[pl.ds(h, 16, heads), :]
    for p in range(PQ):
        planes = [
            proj_own[(48 + 3 * p + c) * heads : (49 + 3 * p + c) * heads, :] for c in range(3)
        ]
        for c, plane in enumerate(turned_planes(planes, own_wide)):
            point_t[pl.ds(3 * p + c, heads, 3 * PQ), :] = plane + own_wide[9 + c : 10 + c]
    queries = jnp.transpose(query_t[...])[0:rows].astype(jnp.bfloat16)
    points = jnp.transpose(point_t[...])[0:rows]
    point_parts = in_three(points)
    for c in range(chunks):
        for at in (36, 52, 68):
            for i in range(4):
                placed_t[c, pl.ds(at + i, heads, ROWS), :] = jnp.zeros((heads, 128), jnp.float32)

    for load in pair_loads:
        load.wait()
    bias_t = bias_weight[...]
    for r in range(rows):
        row = dot_nt(bias_t, pair[r]).astype(jnp.bfloat16).astype(jnp.float32)
        for c in range(chunks):
            bias[c, r * heads : (r + 1) * heads, :] = row[:, c * 128 : (c + 1) * 128]

    loads["local"].wait()
    for c in range(width // 128):
        local_wide[c, 0 : heads * 64, :] = local[:, c * 128 : (c + 1) * 128].astype(jnp.float32)
        local_wide[c, heads * 64 : heads * 64 + 8, :] = jnp.zeros((8, 128), jnp.float32)
    keep = lax.broadcasted_iota(jnp.int32, (16, width), 0) < PV
    for h in range(heads):
        base, at = h * 64, h * FEAT
        local_planes[at : at + 16, :] = local[base : base + 16, :]
        for c in range(3):
            plane = lanes(local_wide, base + 16 + c, 16, 3)
            local_planes[at + 16 * (c + 1) : at + 16 * (c + 2), :] = jnp.where(
                keep, plane, 0.0
            ).astype(jnp.bfloat16)
        plane = lanes(local_wide, base + 52, 16)
        local_planes[at + 64 : at + 80, :] = jnp.where(keep, plane, 0.0).astype(jnp.bfloat16)
    for name in OPERANDS[OPERANDS.index("attended") :]:
        loads[name].wait()
    channels = pair.shape[2]
    row_gain[...] = own_cols[:, 13:14] * (math.sqrt(channels) * pair_gain[...])[None]

    def centre(top, bottom):
        for i in range(top, bottom):
            own_pair = pair[i].astype(jnp.float32)
            centred_pair[i] = own_pair - jnp.mean(own_pair, axis=-1, keepdims=True)

    def project(c):
        lead = c * 128 // rows
        blocks = [buf[m].astype(jnp.float32) for m in range(lead, -(-(c + 1) * 128 // rows))]
        skip = c * 128 - lead * rows
        every = jnp.concatenate(blocks, axis=0)[skip : skip + 128]
        proj_all[c] = dot_nt(proj[...], every.astype(jnp.bfloat16))
        at_lanes = slice(c * 128, (c + 1) * 128)
        turn_here = frames[:, at_lanes]
        key_square = jnp.zeros((heads, 128), jnp.float32)
        for p in range(PQ + PV):
            at = 72 + 3 * p
            planes = [proj_all[c, (at + k) * heads : (at + k + 1) * heads, :] for k in range(3)]
            for k, plane in enumerate(turned_planes(planes, turn_here)):
                plane = plane + turn_here[9 + k : 10 + k]
                plane = plane.astype(jnp.bfloat16).astype(jnp.float32)
                if p < PQ:
                    key_square = key_square + plane * plane
                    slot = 3 * p + k
                else:
                    slot = 24 + 16 * k + p - PQ
                placed_t[c, pl.ds(slot, heads, ROWS), :] = plane
        squares[:, at_lanes] = key_square

    half = pairs // 2
    for step in range(1, half):
        relay(step)
    centre(0, rows)
    for step in range(half, pairs):
        relay(step)
    known = 0
    for c in range(chunks):
        need = min(pairs - 1, ((c + 1) * 128 - 1) // span)
        for step in range(known, need + 1):
            complete(step)
        known = need + 1
        project(c)

    for group in range(0, heads, GROUP):
        members_here = range(group, group + GROUP)
        logits = []
        for h in members_here:
            base = h * ROWS
            keys = lanes(proj_all, 16 * heads + h, 16, heads).astype(jnp.bfloat16)
            key_points = lanes(placed_t, base, 24).astype(jnp.bfloat16)
            query_points = points[:, h * 24 : h * 24 + 24]
            query_square = jnp.sum(query_points * query_points, axis=1, keepdims=True)
            stacked = jnp.concatenate(
                [part[:, h * 24 : h * 24 + 24] for part in point_parts], axis=0
            )
            cross = jnp.dot(stacked, key_points, preferred_element_type=jnp.float32)
            cross = cross[2 * rows : 3 * rows] + cross[rows : 2 * rows] + cross[0:rows]
            distance = query_square + squares[h : h + 1, :] - 2.0 * cross
            scalar = jnp.dot(
                queries[:, h * 16 : h * 16 + 16], keys, preferred_element_type=jnp.float32
            )
            logit = LOGIT_FACTOR * (
                scalar * (1.0 / math.sqrt(HEAD_FEATURES))
                + lanes(bias, h, rows, heads)
                + chain_offset[h] * within
                - (0.5 * math.sqrt(2.0 / (9.0 * PQ)) * distance_weight[h]) * distance
            )
            logits.append(jnp.where(present, logit, -1000000000.0))
        peaks = [jnp.max(logit, axis=1, keepdims=True) for logit in logits]
        exponents = [jnp.exp(logit - peak) for logit, peak in zip(logits, peaks)]
        sums = [jnp.sum(exponent, axis=1, keepdims=True) for exponent in exponents]
        attended_by = [
            (exponent / amount).astype(jnp.bfloat16) for exponent, amount in zip(exponents, sums)
        ]
        for h, weights in zip(members_here, attended_by):
            wide = weights.astype(jnp.float32)
            for c in range(chunks):
                attn[c, pl.ds(h, rows, heads), :] = wide[:, c * 128 : (c + 1) * 128]
        results = []
        for h, weights in zip(members_here, attended_by):
            values = lanes(proj_all, 32 * heads + h, 16, heads)
            stack = jnp.concatenate([values, lanes(placed_t, h * ROWS + 24, 48)], axis=0)
            results.append(dot_nt(stack.astype(jnp.bfloat16), weights))
        for h, result in zip(members_here, results):
            at = h * FEAT
            features[at : at + 16, 0:rows] = result[0:16]
            centred = [
                result[16 * (c + 1) : 16 * (c + 2)] - own[9 + c : 10 + c] for c in range(3)
            ]
            placed = turned_planes(centred, own, transpose=True)
            square = placed[0] * placed[0] + placed[1] * placed[1] + placed[2] * placed[2]
            for c in range(3):
                features[at + 16 * (c + 1) : at + 16 * (c + 2), 0:rows] = placed[c]
            features[at + 64 : at + 80, 0:rows] = jnp.sqrt(square + 1.0)

    for r in range(rows):
        weights = lanes(attn, r * heads, heads).astype(jnp.bfloat16)
        pair_rows[r * heads : (r + 1) * heads, :] = jnp.dot(
            weights, pair[r], preferred_element_type=jnp.float32
        )
    update = exact_dot(jnp.transpose(features[...])[0:rows], local_planes[...])
    attended_rows = jnp.concatenate(
        [pair_rows[pl.ds(h, rows, heads), :] for h in range(heads)], axis=1
    )
    update = update + exact_dot(attended_rows, attended[...])
    updated = layer_norm(single[...].astype(jnp.float32) + update, norm_gain[...][None])
    updated = updated.astype(jnp.bfloat16)
    right_own[...] = jnp.dot(
        updated, right_weight[...], preferred_element_type=jnp.float32
    ).astype(jnp.bfloat16)
    share, arrived, settle = share_block(right_own, right_buf, send_c, recv_c)
    share()
    single_out[...] = updated
    left = jnp.dot(updated, left_weight[...], preferred_element_type=jnp.float32)
    left = left.astype(jnp.bfloat16).astype(jnp.float32)
    left_rows[...] = left - jnp.mean(left, axis=-1, keepdims=True)

    motion = dot_nt(velocity_weight[...], updated)
    ratio = 1.0 / (STEPS - timestep[...]).astype(jnp.float32)
    live = own[13:14]
    turn_vec = ratio * jnp.tanh(motion[0:3]) * live
    speed = ratio * motion[3:6] * live
    x, y, z = turn_vec[0:1], turn_vec[1:2], turn_vec[2:3]
    angle = x * x + y * y + z * z
    coefs = [jnp.zeros_like(angle)] * 3
    powers = jnp.ones_like(angle)
    for order in range(8):
        parity = (-1.0) ** order
        coefs = [
            coef + powers * (parity / float(math.factorial(2 * order + 1 + i)))
            for i, coef in enumerate(coefs)
        ]
        powers = powers * angle
    zero = jnp.zeros_like(angle)
    cross_mat = [[zero, -z, y], [z, zero, -x], [-y, x, zero]]
    times = lambda p, q: [
        [sum(p[a][b] * q[b][c] for b in range(3)) for c in range(len(q[0]))] for a in range(3)
    ]
    squared = times(cross_mat, cross_mat)
    mix = lambda first, second: [
        [
            (1.0 if a == b else 0.0) + first * cross_mat[a][b] + second * squared[a][b]
            for b in range(3)
        ]
        for a in range(3)
    ]
    turn = mix(coefs[0], coefs[1])
    jacobian = mix(coefs[1], coefs[2])
    own_rot = [[own[3 * a + b : 3 * a + b + 1] for b in range(3)] for a in range(3)]
    new_rot = times(own_rot, turn)
    moved = times(own_rot, times(jacobian, [[speed[a : a + 1]] for a in range(3)]))
    for a in range(3):
        for b in range(3):
            rot_out[a, b : b + 1, :] = new_rot[a][b]
        trans_out[a : a + 1, :] = own[9 + a : 10 + a] + moved[a][0]
    drain()

    def prepare(step):
        at = pl.ds(step * span, span)
        arrived(step)
        right = jnp.concatenate([right_buf[2 * step], right_buf[2 * step + 1]], axis=0)
        right = right.astype(jnp.float32)
        right = right - jnp.mean(right, axis=-1, keepdims=True)
        live = live_wide[at, :]
        late = step - (pairs - LATE)
        into = normed.at[step % 2] if late < 0 else left_over.at[late]
        for i in range(rows):
            centred = centred_pair[i, at, :] + (left_rows[i : i + 1, :] + right)
            spread = jnp.sum(centred * centred, axis=-1, keepdims=True) + channels * 1e-05
            scaled = centred * (lax.rsqrt(spread) * live) * row_gain[i : i + 1, :]
            into[i * span : (i + 1) * span, :] = scaled.astype(jnp.bfloat16)
        if late >= 0:
            pair_out[:, at, :] = pair[:, at, :]

    prepare(0)
    for step in range(pairs - LATE):
        prepare(step + 1)
        if step + 1 == pairs - LATE:
            for late in range(step + 2, pairs):
                prepare(late)
        at = step * span
        add_branch(normed.at[step % 2], pair, pair_out, at, span, first, middle, back)
    settle()


def add_branch(normed, pair, out, at, span, first, middle, back, out_at=None):
    rows = pair.shape[0]
    part = rows // PARTS
    out_at = at if out_at is None else out_at
    for top in range(0, rows, part):
        hidden = normed[top * span : (top + part) * span, :]
        hidden = jnp.dot(hidden, first[...], preferred_element_type=jnp.float32)
        hidden = jnp.maximum(hidden.astype(jnp.bfloat16), 0)
        hidden = jnp.dot(hidden, middle[...], preferred_element_type=jnp.float32)
        hidden = jnp.maximum(hidden.astype(jnp.bfloat16), 0)
        branch = jnp.dot(hidden, back[...], preferred_element_type=jnp.float32)
        for i in range(top, top + part):
            added = branch[(i - top) * span : (i - top + 1) * span]
            own_pair = pair[i, pl.ds(at, span), :].astype(jnp.float32)
            out[i, pl.ds(out_at, span), :] = (own_pair + added).astype(jnp.bfloat16)


def deliver_kernel(
    single,
    rot,
    trans,
    pair,
    left_over,
    first,
    middle,
    back,
    single_out,
    rot_out,
    trans_out,
    pair_out,
    block,
    sems,
):
    _, chip, _ = position()
    span = 2 * pair.shape[0]
    pairs = pair.shape[1] // span

    def place(src, step):
        return pltpu.make_async_copy(
            src, pair_out.at[:, chip_columns(chip, step, span), :], sems.at[step]
        )

    copies = [place(pair.at[:, pl.ds(s * span, span), :], s) for s in range(pairs - LATE)]
    copies += [
        pltpu.make_async_copy(src, dst, sems.at[pairs + i])
        for i, (src, dst) in enumerate(
            [(single, single_out), (rot, rot_out), (trans, trans_out)]
        )
    ]
    for copy in copies:
        copy.start()
    for late in range(LATE):
        step = pairs - LATE + late
        into = block.at[late]
        add_branch(left_over.at[late], pair, into, step * span, span, first, middle, back, 0)
        last = place(into, step)
        last.start()
        copies.append(last)
    for copy in copies:
        copy.wait()


def deliver(*arrays):
    rows, cols, channels = arrays[3].shape
    pairs = cols // (2 * rows)
    return pl.pallas_call(
        deliver_kernel,
        out_shape=[jax.ShapeDtypeStruct(a.shape, a.dtype) for a in arrays[:4]],
        in_specs=[pl.BlockSpec(memory_space=pltpu.VMEM)] * len(arrays),
        out_specs=[pl.BlockSpec(memory_space=pl.ANY)] * 4,
        scratch_shapes=[
            pltpu.VMEM((LATE, rows, 2 * rows, channels), arrays[3].dtype),
            pltpu.SemaphoreType.DMA((pairs + 3,)),
        ],
        name="deliver",
    )(*[pltpu.with_memory_space_constraint(a, pltpu.VMEM) for a in arrays])


def run_step(
    single,
    pair,
    rotations,
    translations,
    chain,
    mask,
    timestep,
    proj,
    bias_weight,
    distance_weight,
    chain_offset,
    local,
    attended,
    norm_gain,
    velocity_weight,
    left_weight,
    right_weight,
    pair_gain,
    first,
    middle,
    back,
):
    rows, width = single.shape
    total = rotations.shape[2]
    members = total // rows
    pairs = members // 2
    heads = proj.shape[1]
    channels = pair.shape[2]
    chunks = total // 128
    proj_t = jnp.transpose(proj, (2, 1, 0)).reshape(-1, width)
    operands = dict(
        timestep=timestep.reshape(1, 1),
        distance_weight=distance_weight,
        chain_offset=chain_offset,
        single=single,
        rotations=rotations,
        translations=translations,
        chain=chain,
        mask=mask,
        bias_weight=jnp.transpose(bias_weight),
        norm_gain=norm_gain,
        velocity_weight=jnp.transpose(velocity_weight),
        left_weight=left_weight,
        right_weight=right_weight,
        proj=proj_t,
        pair=pair,
        local=local.reshape(-1, width),
        attended=attended.reshape(-1, width),
        pair_gain=pair_gain,
        first=first,
        middle=middle,
        back=back,
    )
    operands = [operands[name] for name in OPERANDS]
    bf16, f32 = jnp.bfloat16, jnp.float32
    scratch = [
        ((members, rows, width), bf16),
        ((members, rows, channels), bf16),
        ((rows, channels), bf16),
        ((16, total), f32),
        ((total, 16), f32),
        ((chunks, proj_t.shape[0], 128), f32),
        ((proj_t.shape[0], 128), f32),
        ((heads * 16, 128), f32),
        ((heads * 3 * PQ, 128), f32),
        ((chunks, heads * ROWS, 128), f32),
        ((heads, total), f32),
        ((chunks, rows * heads, total // chunks), f32),
        ((chunks, rows * heads, total // chunks), f32),
        ((width // 128, heads * 64 + 8, 128), f32),
        ((heads * FEAT, width), bf16),
        ((heads * FEAT, 128), f32),
        ((rows * heads, channels), f32),
        ((rows, channels), f32),
        ((rows, channels), f32),
        ((total, channels), f32),
        (pair.shape, f32),
        ((2, 2 * rows * rows, channels), bf16),
    ]
    dma = pltpu.SemaphoreType.DMA
    results = pl.pallas_call(
        step_kernel,
        out_shape=(
            pltpu.VMEM((rows, width), bf16),
            pltpu.VMEM((3, 3, rows), f32),
            pltpu.VMEM((3, rows), f32),
            pltpu.VMEM(pair.shape, bf16),
            pltpu.VMEM((LATE, 2 * rows * rows, channels), bf16),
            *[pltpu.VMEM(a.shape, a.dtype) for a in operands[-3:]],
        ),
        in_specs=[pl.BlockSpec(memory_space=pl.ANY)] * len(operands),
        out_specs=(pl.BlockSpec(memory_space=pltpu.VMEM),) * 8,
        scratch_shapes=[pltpu.SMEM(a.shape, a.dtype) for a in operands[:SCALARS]]
        + [pltpu.VMEM(a.shape, a.dtype) for a in operands[SCALARS:-3]]
        + [pltpu.VMEM(*item) for item in scratch]
        + [dma((len(operands),)), dma((pairs,))]
        + [dma((pairs,))] * 4
        + [dma((members,))] * 2,
        compiler_params=pltpu.CompilerParams(collective_id=2, has_side_effects=True),
        name="step",
    )(*operands)
    return deliver(*results)


def shards(
    single,
    pair,
    rotations,
    translations,
    residue_chain_index,
    residue_move_mask,
    timestep,
    single_projection_weight,
    head_bias_weight,
    head_distance_weight,
    chain_logit_offset,
    local_output_weight,
    pair_output_weight,
    single_norm_gain,
    frame_velocity_weight,
    left_pair_weight,
    right_pair_weight,
    pair_norm_gain,
    transition_hidden_weight,
    transition_middle_weight,
    transition_back_weight,
):
    rows_dev = single.shape[0]
    col_count = pair.shape[1]
    total = rotations.shape[2]
    heads_here = single_projection_weight.shape[1]
    row_start = lax.axis_index("res") * rows_dev
    col_start = lax.axis_index("head") * col_count
    pairs = total // rows_dev // 2
    if col_count == total and pairs & (pairs - 1) == 0 and pairs > LATE and rows_dev % 8 == 0:
        return tuple(
            run_step(
                single,
                pair,
                rotations,
                translations,
                residue_chain_index,
                residue_move_mask,
                timestep,
                single_projection_weight,
                head_bias_weight,
                head_distance_weight,
                chain_logit_offset,
                local_output_weight,
                pair_output_weight,
                single_norm_gain,
                frame_velocity_weight,
                left_pair_weight,
                right_pair_weight,
                pair_norm_gain,
                transition_hidden_weight,
                transition_middle_weight,
                transition_back_weight,
            )
        )
    rot_all = jnp.transpose(rotations, (2, 0, 1))
    trans_all = jnp.transpose(translations)
    rot_own = lax.dynamic_slice_in_dim(rot_all, row_start, rows_dev, 0)
    trans_own = lax.dynamic_slice_in_dim(trans_all, row_start, rows_dev, 0)
    own_chain = lax.dynamic_slice_in_dim(residue_chain_index, row_start, rows_dev, 0)
    offset = 3 * HEAD_FEATURES
    feat_count = 2 * HEAD_FEATURES + 3 * PQ + 3 * PV
    members = total // rows_dev
    every_single = gather_blocks(single, members, 0).reshape(total, -1)
    every_proj = jnp.einsum(
        "nd,dhf->nhf", every_single, single_projection_weight, preferred_element_type=jnp.float32
    )
    projected = lax.dynamic_slice_in_dim(every_proj, row_start, rows_dev, 0)
    packed_projection = key_features(every_proj, rot_all, trans_all)
    packed_projection = packed_projection.reshape(total, heads_here, feat_count)
    query_values = projected[:, :, 0:HEAD_FEATURES].astype(jnp.bfloat16)
    query_flattened = to_global(
        projected[:, :, offset : offset + 3 * PQ], rot_own, trans_own, PQ
    ).reshape(rows_dev, heads_here, 3 * PQ)
    bias_local = jnp.einsum(
        "rjc,ch->rhj", pair, head_bias_weight, preferred_element_type=jnp.float32
    ).astype(jnp.bfloat16)
    pair_head_bias = lax.all_to_all(
        bias_local, "head", split_axis=1, concat_axis=2, tiled=True
    ).astype(jnp.float32)
    within_chain = (own_chain[:, None] == residue_chain_index[None, :]).astype(jnp.float32)
    logit_matrix = local_logit_rows(
        query_values,
        query_flattened,
        packed_projection,
        pair_head_bias,
        within_chain,
        head_distance_weight,
        chain_logit_offset,
        residue_move_mask > 0,
    )
    peak = jnp.max(logit_matrix, axis=-1, keepdims=True)
    exponent = jnp.exp(logit_matrix - peak)
    attention = rounded(exponent / jnp.sum(exponent, axis=-1, keepdims=True))
    scalar_out = jnp.einsum(
        "rhn,nhc->rhc",
        attention,
        packed_projection[:, :, HEAD_FEATURES : 2 * HEAD_FEATURES],
        preferred_element_type=jnp.float32,
    )
    point_global = jnp.einsum(
        "rhn,nhp->rhp",
        attention.astype(jnp.float32),
        packed_projection[:, :, 2 * HEAD_FEATURES + 3 * PQ :].astype(jnp.float32),
        precision=HIGHEST,
    )
    update_local = local_points(scalar_out, point_global, rot_own, trans_own, local_output_weight)
    attention_cols = lax.all_to_all(attention, "head", split_axis=2, concat_axis=1, tiled=True)
    pair_attended = jnp.einsum(
        "rhj,rjc->rhc", attention_cols, pair, preferred_element_type=jnp.float32
    )
    update_pair = jnp.einsum(
        "rhc,hcd->rd", pair_attended, pair_output_weight.astype(jnp.float32), precision=HIGHEST
    )
    update = lax.psum(update_local + update_pair, "head")
    single_out = layer_norm(single.astype(jnp.float32) + update, single_norm_gain).astype(
        jnp.bfloat16
    )
    live_all = (residue_move_mask > 0).astype(jnp.float32)
    live_own = lax.dynamic_slice_in_dim(live_all, row_start, rows_dev, 0)
    step_ratio = 1.0 / (STEPS - timestep[0]).astype(jnp.float32)
    rot_out, trans_out = frame_step(
        single_out, frame_velocity_weight, rot_own, trans_own, live_own, step_ratio
    )
    left_proj = jnp.dot(single_out, left_pair_weight, preferred_element_type=jnp.float32).astype(
        jnp.bfloat16
    )
    own_right = jnp.dot(single_out, right_pair_weight, preferred_element_type=jnp.float32).astype(
        jnp.bfloat16
    )
    every_right = gather_blocks(own_right, members, 1).reshape(total, -1)
    right_proj = lax.dynamic_slice_in_dim(every_right, col_start, col_count, 0)
    (pair_out,) = run_transition(
        residue_move_mask,
        pair,
        left_proj.astype(jnp.float32),
        right_proj.astype(jnp.float32),
        lax.dynamic_slice_in_dim(residue_move_mask, col_start, col_count, 0),
        pair_norm_gain,
        transition_hidden_weight,
        transition_middle_weight,
        transition_back_weight,
    )
    return (single_out, rot_out, trans_out, pair_out)


def solution(mesh):
    placed = (
        P(("batch", "res"), None),
        P(("batch", "res"), "head", None),
        P(None, None, "batch"),
        P(None, "batch"),
        P(),
        P("batch"),
        P(),
        P(None, "head", None),
        P(),
        P("head"),
        P("head"),
        P("head", None, None),
        P(),
        P(),
        P(),
        P(),
        P(),
        P(),
        P(),
        P(),
        P(),
    )
    return jax.shard_map(
        shards,
        mesh=mesh,
        in_specs=placed,
        out_specs=(
            P(("batch", "res"), None),
            P(None, None, ("batch", "res")),
            P(None, ("batch", "res")),
            P(("batch", "res"), "head", None),
        ),
        check_vma=False,
    )
```
